32 devices in a mesh: dp: 4 (over y, x), expert: 8 (over z, core).
Axes of the slice: x: 2, y: 2, z: 4, core: 2. Of those that a mesh axis runs over, the one named last changes fastest.
Arguments:
- conv_cache: float32 [128, 3, 16384], P('dp', None, 'expert'), may hold values from -6 to 6
- state_cache: float32 [128, 16, 16384], P('dp', None, 'expert'), may hold values from -6 to 6
- send_slot: int32 [4, 4, 8], replicated, may hold values from 0 to 31, as said below
- recv_row: int32 [4, 4, 8], P('dp'), may hold values from 0 to 31, as said below
- prefix_length: int32 [128], P('dp'), may hold values from 1 to 4
- x_input: bfloat16 [2, 128, 16384], P(None, 'dp', 'expert'), may hold values from -6 to 6
- z_input: bfloat16 [2, 128, 16384], P(None, 'dp', 'expert'), may hold values from -6 to 6
- dt_input: bfloat16 [2, 128, 16384], P(None, 'dp', 'expert'), may hold values from -6 to 6
- b_input: float32 [2, 128, 16], P(None, 'dp'), may hold values from -6 to 6
- c_input: float32 [2, 128, 16], P(None, 'dp'), may hold values from -4 to 4
- conv_weight: float32 [4, 16384], P(None, 'expert'), may hold values from -3 to 3
- conv_bias: float32 [16384], P('expert'), may hold values from -3 to 3
- dt_bias: float32 [16384], P('expert'), may hold values from -3 to 1
- decay_rate: float32 [16, 16384], P(None, 'expert'), may hold values from 0.02 to 4
- skip_gain: float32 [16384], P('expert'), may hold values from 0.5 to 1.5
- out_weight: bfloat16 [16384, 8192], P('expert', 'dp'), may hold values from -0.046875 to 0.046875
- norm_gain: float32 [8192], replicated, may hold values from 0.25 to 1.75
- route_ids: int32 [2, 128, 2], replicated, may hold values from 0 to 15, all different within a row; in each aligned block of 256 rows (0 to 255, 256 to 511, ..., all dimensions but the last counted through in order) at most 64 rows name the same one
- route_weight: float32 [2, 128, 2], replicated, may hold values from 0.2 to 1
- expert_slots: int32 [4], replicated, may hold values from 0 to 15, as said below
- gate_weight: bfloat16 [8192, 49152], P(None, ('dp', 'expert')), may hold values from -0.0625 to 0.0625
- up_weight: bfloat16 [8192, 49152], P(None, ('dp', 'expert')), may hold values from -0.0625 to 0.0625
- down_weight: bfloat16 [49152, 8192], P(('dp', 'expert')), may hold values from -0.0546875 to 0.0546875
Outputs:
- mixed: bfloat16 [256, 8192], P(('dp', 'expert'))
- new_state: float32 [128, 16, 16384], P('dp', None, 'expert')
- new_tail: float32 [128, 3, 16384], P('dp', None, 'expert')
The draws below stay inside these ranges and needn't reach their ends.
Inputs may be any that keep to these rules, and one draw needn't show every extreme that they name: For each owner o, send_slot[o] holds every local slot 0 to 31 exactly once. For each index d, recv_row[d] holds every local row 0 to 31 exactly once. `route_ids`: over both steps and all rows, no expert is named by more than 64 rows, and one is named by exactly 64. `expert_slots`: distinct expert ids; experts 0 and 15 are always among them, in slots that vary.
All inputs are finite; a program needn't handle non-finite values.
Results may differ from the reference program's by a relative error of at most 0.0057.
Values may be sent and summed in bfloat16 or wider, within the bound.
No kernel may reach another device: no remote copies, remote signals or barrier semaphores. Data moves between devices by JAX's collectives and lax.ppermute only.
A program may use at most 256 MiB of HBM per device.

```python
import math
import jax
import jax.numpy as jnp
import numpy as np
from jax import lax

D = 8192
DI = 16384
NS = 16
CONV = 4
EXPERTS = 16
TOPK = 2
FFW = 12288
EF = 4
STEPS = 2
R_DP = 32
ROWS = 128
PER = 8
CAP = 64
N_DP = 4


def owner_lists(key):
    keys = jax.random.split(key, N_DP)
    perms = jax.vmap(lambda single: jax.random.permutation(single, R_DP))(keys)
    return perms.reshape(N_DP, N_DP, PER).astype(jnp.int32)


def draw_send_slot(key, part):
    return owner_lists(jax.random.fold_in(key, 11))


def draw_recv_row(key, part):
    return owner_lists(jax.random.fold_in(key, 23))


def draw_expert_slots(key, part):
    middle = jax.random.permutation(jax.random.fold_in(key, 37), EXPERTS - 2)[:EF - 2].astype(jnp.int32) + 1
    chosen = jnp.concatenate([jnp.array([0, EXPERTS - 1], jnp.int32), middle])
    return jax.random.permutation(jax.random.fold_in(key, 41), chosen).astype(jnp.int32)


def set_ends(values, rng, smallest, largest):
    longest = values.shape.index(max(values.shape))
    spots = []
    for shift in (0, 1):
        where = [jax.random.randint(jax.random.fold_in(rng, axis), (), 0, length) for axis, length in enumerate(values.shape)]
        where[longest] = (where[longest] + shift) % values.shape[longest]
        spots.append(tuple(where))
    return values.at[spots[0]].set(smallest).at[spots[1]].set(largest)


def steps_of(own_key, extent, cuts, least, top_value):
    loudness = 1.0
    for dim, parts in cuts:
        draws = jax.random.uniform(jax.random.fold_in(jax.random.fold_in(own_key, 6), dim), (parts,), jnp.float32, least / len(cuts), top_value / len(cuts))
        loudness = loudness * jnp.repeat(jnp.exp(draws), extent[dim] // parts).reshape((-1,) + (1,) * (len(extent) - 1 - dim))
    return loudness


def deal_out(rng, own, number, rows, count, top, most, skew):
    order = jax.random.permutation(rng, count)
    packed, ordinary = portions_of(count, rows * top, most, skew, True), portions_of(count, rows * top, most, skew, False)
    places = jnp.arange(count)

    def named(tallies, rotation):
        used = int((tallies > 0).sum())
        fixed = max(1, used // 4)
        shifted = fixed + (places - fixed + rotation * (used - fixed)) % max(1, count - fixed)
        return jnp.zeros((count,), jnp.int32).at[order[jnp.where(places < fixed, places, shifted)]].set(jnp.asarray(tallies, jnp.int32))

    tallies = jnp.where(number % 4 == 0, named(packed, number // 4), named(ordinary, number - number // 4 - 1))
    mixed = jax.random.permutation(jax.random.fold_in(own, 3), count)
    source_of, taker = mixed[0:count // 2 * 2:2], mixed[1:count // 2 * 2:2]
    slack = jnp.minimum(tallies[source_of] - 1, most - tallies[taker]) // 2
    slack = jnp.where((source_of == order[0]) | (taker == order[0]) | (tallies[taker] == 0), 0, jnp.maximum(slack, 0))
    shifted = jax.random.randint(jax.random.fold_in(own, 4), (count // 2,), 0, 1 << 20) % (slack + 1)
    tallies = tallies.at[source_of].add(-shifted).at[taker].add(shifted)
    members = jnp.searchsorted(jnp.cumsum(tallies), jnp.arange(rows * top), side="right").astype(jnp.int32)
    listing = members.reshape(top, rows).T
    listing = listing[jax.random.permutation(jax.random.fold_in(own, 1), rows)]
    rotation = jax.random.randint(jax.random.fold_in(own, 2), (rows, 1), 0, top)
    return jnp.take_along_axis(listing, (jnp.arange(top)[None, :] + rotation) % top, axis=1)


def portions_of(count, total, limit, slope, full):
    loads = [(1 << 20) // math.isqrt(grade ** slope) + 1 for grade in range(1, count + 1)]
    largest = limit if full else min(limit, max(-(-total // count), total * loads[0] // sum(loads)))
    least = 1 if total - largest >= count - 1 else 0
    given, rest = [largest] + [least] * (count - 1), total - largest - least * (count - 1)
    while rest > 0:
        candidates = [i for i in range(1, count) if given[i] < largest] or [i for i in range(1, count) if given[i] < limit]
        whole, budget = sum([loads[i] for i in candidates]), rest
        for i in candidates:
            more = min(limit - given[i], max(1, budget * loads[i] // whole), rest)
            given[i] = given[i] + more
            rest = rest - more
    return np.array(given)


def centred(rng, extent, width, bound, cuts=(), kind=jnp.bfloat16):
    result = width * jax.random.normal(rng, extent, jnp.float32)
    if cuts:
        result = result * steps_of(rng, extent, cuts, -0.22, 0.18)
    return jnp.clip(result, -bound, bound).astype(kind)


def setup_inputs(seed: int = 0) -> dict:
    streams_of = jax.random.split(jax.random.key(seed), 24)
    conv_cache = centred(streams_of[0], (ROWS, CONV - 1, DI), 1.0, 6.0, ((0, 4), (2, 8)), jnp.float32)
    state_cache = centred(streams_of[1], (ROWS, NS, DI), 1.0, 6.0, ((0, 4), (2, 8)), jnp.float32)
    send_slot = draw_send_slot(jax.random.fold_in(streams_of[23], 71), 0)
    recv_row = draw_recv_row(jax.random.fold_in(streams_of[23], 71), 0)
    prefix_length = set_ends(jax.random.randint(streams_of[4], (ROWS,), 1, 5), jax.random.fold_in(streams_of[4], 1), 1, 4).astype(jnp.int32)
    x_input = centred(streams_of[5], (STEPS, ROWS, DI), 1.0, 6.0, ((1, 4), (2, 8)))
    z_input = centred(streams_of[6], (STEPS, ROWS, DI), 1.0, 6.0, ((1, 4), (2, 8)))
    dt_input = centred(streams_of[7], (STEPS, ROWS, DI), 1.0, 6.0, ((1, 4), (2, 8)))
    b_input = centred(streams_of[8], (STEPS, ROWS, NS), 1.0, 6.0, ((1, 4),), jnp.float32)
    c_input = centred(streams_of[9], (STEPS, ROWS, NS), 0.5, 4.0, ((1, 4),), jnp.float32)
    conv_weight = centred(streams_of[10], (CONV, DI), 0.5, 3.0, ((1, 8),), jnp.float32)
    conv_bias = centred(streams_of[11], (DI,), 0.5, 3.0, ((0, 8),), jnp.float32)
    dt_bias = jnp.clip(-3.0 + 4.0 * jax.random.uniform(streams_of[12], (DI,), jnp.float32) ** steps_of(streams_of[12], (DI,), ((0, 8),), -0.2, 0.2), -3.0, 1.0)
    decay_rate = jnp.clip(jnp.exp(math.log(4.0) - 5.2983174 * jax.random.uniform(streams_of[13], (NS, DI), jnp.float32) ** steps_of(streams_of[13], (NS, DI), ((1, 8),), -0.2, 0.2)), 0.02, 4.0)
    skip_gain = jnp.clip(0.5 + 1.0 * jax.random.uniform(streams_of[14], (DI,), jnp.float32) ** steps_of(streams_of[14], (DI,), ((0, 8),), -0.2, 0.2), 0.5, 1.5)
    out_weight = centred(streams_of[15], (DI, D), DI ** -0.5, 0.046875, ((0, 8), (1, 4)))
    norm_gain = jnp.clip(1.0 + 0.15 * jax.random.normal(streams_of[16], (D,), jnp.float32), 0.25, 1.75)
    route_ids_keys = jax.random.split(jax.random.fold_in(streams_of[17], 1), STEPS * ROWS // (STEPS * ROWS))
    route_ids_turns = jax.random.permutation(jax.random.fold_in(streams_of[17], 3), STEPS * ROWS // (STEPS * ROWS))
    route_ids = jax.vmap(lambda own, number: deal_out(jax.random.fold_in(streams_of[17], 2), own, number, STEPS * ROWS, EXPERTS, TOPK, CAP, 2))(route_ids_keys, route_ids_turns).reshape((STEPS, ROWS, TOPK))
    route_weight = jnp.clip(jax.random.uniform(streams_of[18], (STEPS, ROWS, TOPK), jnp.float32, 0.2, 1.0), 0.2, 1.0)
    expert_slots = draw_expert_slots(jax.random.fold_in(streams_of[23], 71), 0)
    gate_weight = centred(streams_of[20], (D, EF * FFW), D ** -0.5, 0.0625, ((1, 32),))
    up_weight = centred(streams_of[21], (D, EF * FFW), D ** -0.5, 0.0625, ((1, 32),))
    down_weight = centred(streams_of[22], (EF * FFW, D), FFW ** -0.5, 0.0546875, ((0, 32),))
    return {"conv_cache": conv_cache, "state_cache": state_cache, "send_slot": send_slot, "recv_row": recv_row, "prefix_length": prefix_length, "x_input": x_input, "z_input": z_input, "dt_input": dt_input, "b_input": b_input, "c_input": c_input, "conv_weight": conv_weight, "conv_bias": conv_bias, "dt_bias": dt_bias, "decay_rate": decay_rate, "skip_gain": skip_gain, "out_weight": out_weight, "norm_gain": norm_gain, "route_ids": route_ids, "route_weight": route_weight, "expert_slots": expert_slots, "gate_weight": gate_weight, "up_weight": up_weight, "down_weight": down_weight}


def reference(conv_cache, state_cache, send_slot, recv_row, prefix_length, x_input, z_input, dt_input, b_input, c_input, conv_weight, conv_bias, dt_bias, decay_rate, skip_gain, out_weight, norm_gain, route_ids, route_weight, expert_slots, gate_weight, up_weight, down_weight):
    owners = jnp.arange(N_DP, dtype=jnp.int32)
    dest_rows = (owners[:, None, None] * R_DP + recv_row).reshape(-1).astype(jnp.int32)
    source_slots = (owners[None, :, None] * R_DP + jnp.transpose(send_slot, (1, 0, 2))).reshape(-1).astype(jnp.int32)
    source = jnp.zeros((ROWS,), jnp.int32).at[dest_rows].set(source_slots)
    tail = conv_cache[source]
    state = state_cache[source]
    offsets = CONV - 1 - jnp.arange(CONV - 1, dtype=jnp.int32)
    valid = (offsets[None, :] <= prefix_length[:, None]).astype(jnp.float32)
    tail = tail * valid[:, :, None]
    outputs = []
    for step in range(STEPS):
        window = jnp.concatenate([tail, x_input[step].astype(jnp.float32)[:, None, :]], axis=1)
        xc = jax.nn.silu(lax.optimization_barrier(jnp.sum(window * conv_weight[None], axis=1)) + conv_bias)
        tail = window[:, 1:, :]
        delta = jax.nn.softplus(dt_input[step].astype(jnp.float32) + dt_bias)
        state = jnp.exp(-delta[:, None, :] * decay_rate[None]) * state + (delta * xc)[:, None, :] * b_input[step][:, :, None]
        out_y = lax.optimization_barrier(jnp.sum(c_input[step][:, :, None] * state, axis=1)) + skip_gain * xc
        out_y = out_y * jax.nn.silu(z_input[step].astype(jnp.float32))
        outputs.append(out_y.astype(jnp.bfloat16))
    y_all = jnp.stack(outputs).reshape(STEPS * ROWS, DI)
    hidden = jnp.dot(y_all, out_weight, preferred_element_type=jnp.float32).astype(jnp.bfloat16)
    hidden_f = hidden.astype(jnp.float32)
    normed = (hidden_f * lax.rsqrt(lax.optimization_barrier(jnp.mean(hidden_f * hidden_f, axis=-1, keepdims=True)) + 1e-05) * norm_gain).astype(jnp.bfloat16)
    ids = route_ids.reshape(STEPS * ROWS, TOPK)
    weights = route_weight.reshape(STEPS * ROWS, TOPK)
    share = lax.optimization_barrier(jnp.sum(weights[:, :, None] * (ids[:, :, None] == expert_slots[None, None, :]).astype(jnp.float32), axis=1))

    def add_slot(slot, total):
        begin = (slot * FFW).astype(jnp.int32)
        gate_cols = lax.dynamic_slice_in_dim(gate_weight, begin, FFW, 1)
        up_cols = lax.dynamic_slice_in_dim(up_weight, begin, FFW, 1)
        down_rows = lax.dynamic_slice_in_dim(down_weight, begin, FFW, 0)
        weight_col = lax.dynamic_slice_in_dim(share, slot.astype(jnp.int32), 1, 1)
        gated = jnp.dot(normed, gate_cols, preferred_element_type=jnp.float32)
        upped = jnp.dot(normed, up_cols, preferred_element_type=jnp.float32)
        act = (jax.nn.silu(gated) * upped * weight_col).astype(jnp.bfloat16)
        return total + jnp.dot(act, down_rows, preferred_element_type=jnp.float32)
    summed = lax.fori_loop(jnp.int32(0), jnp.int32(EF), add_slot, jnp.zeros((STEPS * ROWS, D), jnp.float32))
    mixed = (hidden_f + summed).astype(jnp.bfloat16)
    return (mixed, state, tail)
```

```python
import functools

import jax
import jax.numpy as jnp
from jax import lax
from jax.experimental import pallas as pl
from jax.experimental.pallas import tpu as pltpu
from jax.sharding import Mesh
from jax.sharding import PartitionSpec as P

FFW = 12288
BF = jnp.bfloat16
F32 = jnp.float32
META = 256
TABLE = 96
PREFIX = 64
NT = (((1,), (1,)), ((), ()))
TN = (((0,), (0,)), ((), ()))


def cost(flops, moved):
    return pl.CostEstimate(flops=int(flops), bytes_accessed=int(moved), transcendentals=0)


def params(limit):
    return pltpu.CompilerParams(vmem_limit_bytes=limit << 20)


def iota(shape, dim):
    return lax.broadcasted_iota(jnp.int32, shape, dim)


def trade(piece, axis, size, k):
    return lax.ppermute(piece, axis, [(i, i ^ k) for i in range(size)])


def pack_kernel(n, per, me, rr, x, z, dt, b, c, prefix, *rest):
    outs, m_scr = rest[:n], rest[n]
    steps, rows, ch = x.shape
    states = b.shape[1]
    m_scr[...] = jnp.zeros_like(m_scr)
    for t in range(steps):
        m_scr[2 * t * states : (2 * t + 1) * states, :] = b[t]
        m_scr[(2 * t + 1) * states : (2 * t + 2) * states, :] = c[t]
    m_scr[PREFIX : PREFIX + 1, :] = prefix[...].astype(F32)
    rowcol = jnp.zeros((n * per, 1), jnp.int32)
    table = jnp.zeros((1, 128), F32)
    sub = iota((n * per, 1), 0)
    lane = iota((1, 128), 1)
    for k in range(n):
        for i in range(per):
            rowcol = jnp.where(sub == k * per + i, rr[(me[0] ^ k) * per + i], rowcol)
            q = k * per + i
            table = jnp.where(lane == TABLE + q, rr[q].astype(F32), table)
    hot = rowcol == iota((n * per, rows), 1)
    hot_b = hot.astype(BF)
    for a, src in enumerate((x, z, dt)):
        for t in range(steps):
            got = jnp.dot(hot_b, src[t], preferred_element_type=F32).astype(BF)
            at = (a * steps + t) * ch
            for k in range(n):
                outs[k][:, at : at + ch] = got[k * per : (k + 1) * per]
    meta = lax.dot_general(
        hot.astype(F32), m_scr[...], NT, precision=lax.Precision.HIGHEST, preferred_element_type=F32
    )
    meta = meta + table
    hi = meta.astype(BF)
    lo = (meta - hi.astype(F32)).astype(BF)
    at = 3 * steps * ch
    for k in range(n):
        outs[k][:, at : at + 128] = hi[k * per : (k + 1) * per]
        outs[k][:, at + 128 : at + 256] = lo[k * per : (k + 1) * per]


def ssm_kernel(k, n, per, steps, me, ss, *refs):
    arrs = refs[: 3 * steps]
    meta, par, decay, conv = refs[3 * steps : 3 * steps + 4]
    state = refs[3 * steps + 4 : 3 * steps + 4 + per]
    y_out, st_out, y_scr, tail_scr = refs[-4:]
    taps = conv.shape[0]
    states, cb = decay.shape
    val = meta[:, :128].astype(F32) + meta[:, 128:].astype(F32)
    val_t = jnp.transpose(jnp.concatenate([val, jnp.zeros((128 - per, 128), F32)], axis=0))
    base = (me[0] * n + (me[0] ^ k)) * per
    for j in range(taps):
        for i in range(per):
            tail_scr[j, i : i + 1, :] = conv[j, pl.ds(ss[base + i], 1), :]
    prefix = val[:, PREFIX : PREFIX + 1]
    window = [
        tail_scr[j] * (prefix >= float(taps - j)).astype(F32) for j in range(taps)
    ]
    deltas, us, skips, gates = [], [], [], []
    for t in range(steps):
        window.append(arrs[t][...].astype(F32))
        acc = window[t] * par[0:1, :]
        for j in range(1, taps + 1):
            acc = acc + window[t + j] * par[j : j + 1, :]
        acc = acc + par[taps + 1 : taps + 2, :]
        xc = acc * jax.nn.sigmoid(acc)
        raw = arrs[2 * steps + t][...].astype(F32) + par[taps + 2 : taps + 3, :]
        delta = jnp.maximum(raw, 0.0) + jnp.log1p(jnp.exp(-jnp.abs(raw)))
        zt = arrs[steps + t][...].astype(F32)
        deltas.append(delta)
        us.append(delta * xc)
        skips.append(par[taps + 3 : taps + 4, :] * xc)
        gates.append(zt * jax.nn.sigmoid(zt))
    dec = decay[...]
    for i in range(per):
        st = state[i][0]
        for t in range(steps):
            at = 2 * t * states
            bcol = val_t[at : at + states, i : i + 1]
            ccol = val_t[at + states : at + 2 * states, i : i + 1]
            st = jnp.exp(-(deltas[t][i : i + 1] * dec)) * st + us[t][i : i + 1] * bcol
            y_scr[t, i : i + 1, :] = jnp.sum(ccol * st, axis=0, keepdims=True)
        st_out[i * states : (i + 1) * states, :] = st.astype(st_out.dtype)
    for t in range(steps):
        out = (y_scr[t] + skips[t]) * gates[t]
        y_out[0, t * per : (t + 1) * per, :] = out.astype(BF)
    kept = window[steps:taps]
    low = st_out.shape[0] - per * states
    kept.append(jnp.zeros((low - per * len(kept), cb), F32))
    st_out[per * states :, :] = jnp.concatenate(kept, axis=0).astype(st_out.dtype)


def drop_first(fn):
    return lambda me, ss, alias, *refs: fn(me, ss, *refs)


def ssm(k, n, per, steps, me, ss, payload, par, decay, conv, state, y_buf):
    states, ch = decay.shape
    cb = ch // 4
    blocks = ch // cb
    taps = conv.shape[0]
    low = -(-(taps - steps) * per // 16) * 16
    specs = [
        pl.BlockSpec((per, cb), functools.partial(lambda a, g, *_: (0, a * blocks + g), a))
        for a in range(3 * steps)
    ]
    specs.append(pl.BlockSpec((per, META), lambda g, *_: (0, 3 * steps * ch // META)))
    specs.append(pl.BlockSpec((par.shape[0], cb), lambda g, *_: (0, g)))
    specs.append(pl.BlockSpec((states, cb), lambda g, *_: (0, g)))
    specs.append(pl.BlockSpec((taps, conv.shape[1], cb), lambda g, *_: (0, 0, g)))
    for i in range(per):
        specs.append(
            pl.BlockSpec(
                (1, states, cb),
                functools.partial(
                    lambda i, g, m, s: (s[(m[0] * n + (m[0] ^ k)) * per + i], 0, g), i
                ),
            )
        )
    args = [payload] * (3 * steps + 1) + [par, decay, conv] + [state] * per
    body = functools.partial(ssm_kernel, k, n, per, steps)
    alias = {}
    if y_buf is not None:
        specs = [pl.BlockSpec(memory_space=pl.ANY)] + specs
        args = [y_buf] + args
        body = drop_first(body)
        alias = {2: 0}
    st_type = F32 if k == 0 else BF
    return pl.pallas_call(
        body,
        grid_spec=pltpu.PrefetchScalarGridSpec(
            num_scalar_prefetch=2,
            grid=(blocks,),
            in_specs=specs,
            out_specs=[
                pl.BlockSpec((1, steps * per, cb), lambda g, *_: (k, 0, g)),
                pl.BlockSpec((per * states + low, cb), lambda g, *_: (0, g)),
            ],
            scratch_shapes=[
                pltpu.VMEM((steps, per, cb), F32),
                pltpu.VMEM((taps, per, cb), F32),
            ],
        ),
        out_shape=[
            jax.ShapeDtypeStruct((n, steps * per, ch), BF),
            jax.ShapeDtypeStruct((per * states + low, ch), st_type),
        ],
        input_output_aliases=alias,
        compiler_params=params(24),
        cost_estimate=cost(3e6, 3 << 20),
        name=f"ssm{k}",
    )(me, ss, *args)


def select_kernel(n, m, per, steps, rows, rm, pe, width, me, es, ids, wts, *refs):
    tables = refs[:n]
    sel, share, expand = refs[n:]
    cores = m * 2
    d, zz, cc = me[0], me[1], me[2]
    total = steps * n * rows
    choices = ids.shape[0]
    sub8 = iota((8, total), 0)
    match = jnp.zeros((8, total), F32)
    own_share = jnp.zeros((1, total), F32)
    hits = []
    for kd in range(n):
        eid = es[((d ^ kd) * (cores * width)) // FFW]
        hit = jnp.zeros((1, total), F32)
        for q in range(choices):
            same = ids[q : q + 1, :] == eid
            hit = jnp.where(same, 1.0, hit)
            if kd == 0:
                own_share = own_share + jnp.where(same, wts[q : q + 1, :], 0.0)
        hits.append(hit)
        match = jnp.where(sub8 == kd, hit, match)
    before = (iota((total, total), 0) < iota((total, total), 1)).astype(BF)
    pos = jnp.dot(match.astype(BF), before, preferred_element_type=F32)
    pos = jnp.where(match > 0.0, pos, -1.0)
    col = iota((pe, 1), 0)
    parts = []
    for h in range(2):
        for kz in range(m):
            first = ((zz ^ kz) * 2 + (cc ^ h)) * pe
            want = (col + first).astype(F32)
            for kd in range(n):
                parts.append((pos[kd : kd + 1, :] == want).astype(BF))
        row = iota((m * n * rm, 1), 0)
        kz_v = row // (n * rm)
        kd_v = (row // rm) % n
        true = ((d ^ kd_v) * cores + (zz ^ kz_v) * 2 + (cc ^ h)) * rm + row % rm
        parts.append((true == iota((m * n * rm, total), 1)).astype(BF))
    sel_true = jnp.concatenate(parts, axis=0)
    j = iota((total, 1), 0)
    ko = j // (n * steps * per)
    kd = (j // (steps * per)) % n
    tab = jnp.zeros((8, 128), F32)
    for q in range(n):
        tab = jnp.where(iota((8, 128), 0) == q, tables[q][0:1, :].astype(F32), tab)
    pick = (iota((total, 8), 1) == (ko ^ kd)).astype(BF)
    tj = jnp.dot(pick, tab.astype(BF), preferred_element_type=F32)
    lane = TABLE + (d ^ ko) * per + j % per
    local = jnp.sum(jnp.where(iota((total, 128), 1) == lane, tj, 0.0), axis=1, keepdims=True)
    true = ((j // per) % steps) * (n * rows) + (d ^ ko ^ kd) * rows + local.astype(jnp.int32)
    perm = (true == iota((total, total), 1)).astype(BF)
    sel[...] = lax.dot_general(sel_true, perm, NT, preferred_element_type=F32).astype(BF)
    hot = pos[0:1, :] == iota((cores * pe, 1), 0).astype(F32)
    expand[...] = hot.astype(BF)
    mine = jnp.sum(jnp.where(hot, own_share, 0.0), axis=1, keepdims=True)
    share[...] = jnp.broadcast_to(mine, share.shape)


def project_kernel(n, counts, *refs):
    ys = refs[:n]
    sel, w = refs[n], refs[n + 1]
    outs = refs[n + 2 : n + 2 + len(counts)]
    y_all, y_sel = refs[-2:]

    @pl.when(pl.program_id(0) == 0)
    def _():
        size = ys[0].shape[0]
        for q in range(n):
            y_all[q * size : (q + 1) * size, :] = ys[q][...]
        y_sel[...] = jnp.dot(sel[...], y_all[...], preferred_element_type=F32).astype(BF)

    at = 0
    for out, count in zip(outs, counts):
        out[...] = jnp.dot(
            y_sel[at : at + count, :], w[...], preferred_element_type=F32
        ).astype(BF)
        at += count


def gate_kernel(pieces, me, *refs):
    xs = refs[:pieces]
    share, gw, uw, act, x_scr, g_acc, u_acc = refs[pieces:]
    g = pl.program_id(0)
    pe = xs[0].shape[0]

    @pl.when(g == 0)
    def _():
        first = me[2] == 0
        for kz in range(pieces // 2):
            own, other = xs[2 * kz][...].astype(F32), xs[2 * kz + 1][...].astype(F32)
            pair = jnp.concatenate(
                [jnp.where(first, own, other), jnp.where(first, other, own)], axis=0
            ).astype(BF)
            at = pl.multiple_of((me[1] ^ kz) * (2 * pe), 2 * pe)
            x_scr[pl.ds(at, 2 * pe), :] = pair
        g_acc[...] = jnp.zeros_like(g_acc)
        u_acc[...] = jnp.zeros_like(u_acc)

    kb = gw.shape[0]
    xk = x_scr[:, pl.ds(pl.multiple_of(g * kb, kb), kb)]
    g_acc[...] += jnp.dot(xk, gw[...], preferred_element_type=F32)
    u_acc[...] += jnp.dot(xk, uw[...], preferred_element_type=F32)

    @pl.when(g == pl.num_programs(0) - 1)
    def _():
        gated = g_acc[...]
        act[...] = (gated * jax.nn.sigmoid(gated) * u_acc[...] * share[:, 0:1]).astype(BF)


def down_kernel(me, act, dw, out):
    out[...] = jnp.dot(act[...], dw[...], preferred_element_type=F32).astype(BF)


def place_kernel(states, me, rr, src, *refs):
    out = refs[-1]
    out[0] = src[...].astype(F32)


def place(k, n, per, rows, states, me, rr, src, buf):
    ch = src.shape[1]
    specs = [pl.BlockSpec((states, ch), lambda i, *_: (i, 0))]
    args = [src]
    alias = {}
    if buf is not None:
        specs.append(pl.BlockSpec(memory_space=pl.ANY))
        args.append(buf)
        alias = {3: 0}
    return pl.pallas_call(
        functools.partial(place_kernel, states),
        grid_spec=pltpu.PrefetchScalarGridSpec(
            num_scalar_prefetch=2,
            grid=(per,),
            in_specs=specs,
            out_specs=pl.BlockSpec(
                (1, states, ch), lambda i, m, r: (r[(m[0] ^ k) * per + i], 0, 0)
            ),
        ),
        out_shape=jax.ShapeDtypeStruct((rows, states, ch), F32),
        input_output_aliases=alias,
        compiler_params=params(16),
        cost_estimate=cost(1e5, 2 << 20),
        name=f"place{k}",
    )(me, rr, *args)


def tail_kernel(n, per, taps, me, rr, x, *refs):
    tails, out = refs[:n], refs[n]
    steps = x.shape[0]
    keep = taps - steps
    for t in range(steps):
        out[keep + t] = x[t].astype(F32)
    for k in range(n):
        block = tails[k][...].astype(F32)
        for j in range(keep):
            for i in range(per):
                q = j * per + i
                out[j, pl.ds(rr[(me[0] ^ k) * per + i], 1), :] = block[q : q + 1, :]


def final_kernel(n, m, me, *refs):
    hid = refs[:n]
    parts = refs[n : n + 2 * m]
    out, acc = refs[-2:]
    wc = hid[0].shape[1]
    for k in range(n):
        acc[:, pl.ds(pl.multiple_of((me[0] ^ k) * wc, wc), wc)] = hid[k][...].astype(F32)
    pc = parts[0].shape[1]
    for q in range(2 * m):
        zs, cs = me[1] ^ (q // 2), me[2] ^ (q % 2)
        where = pl.ds(pl.multiple_of((cs * m + zs) * pc, pc), pc)
        acc[:, where] = acc[:, where] + parts[q][...].astype(F32)
    out[...] = acc[...].astype(BF)


def body(
    conv_cache,
    state_cache,
    send_slot,
    recv_row,
    prefix_length,
    x_input,
    z_input,
    dt_input,
    b_input,
    c_input,
    conv_weight,
    conv_bias,
    dt_bias,
    decay_rate,
    skip_gain,
    out_weight,
    norm_gain,
    route_ids,
    route_weight,
    expert_slots,
    gate_weight,
    up_weight,
    down_weight,
):
    n = lax.axis_size("dp")
    m = lax.axis_size("z")
    d, zz, cc = lax.axis_index("dp"), lax.axis_index("z"), lax.axis_index("core")
    me = jnp.stack([d, zz, cc]).astype(jnp.int32)
    steps, rows, ch = x_input.shape
    per = rows // n
    taps = conv_cache.shape[1]
    states = state_cache.shape[1]
    total = steps * n * rows
    cap = total // 4
    pe = cap // (2 * m)
    rm = total // (n * 2 * m)
    width = gate_weight.shape[1]
    wc = out_weight.shape[1]
    dm = n * wc
    rr = recv_row.reshape(-1)
    ss = send_slot.reshape(-1)
    vm = pl.BlockSpec(memory_space=pltpu.VMEM)
    sm = pl.BlockSpec(memory_space=pltpu.SMEM)

    payload = pl.pallas_call(
        functools.partial(pack_kernel, n, per),
        in_specs=[sm, sm] + [vm] * 6,
        out_specs=[vm] * n,
        out_shape=[jax.ShapeDtypeStruct((per, 3 * steps * ch + META), BF)] * n,
        scratch_shapes=[pltpu.VMEM((128, rows), F32)],
        compiler_params=params(16),
        cost_estimate=cost(1e6, 2 << 20),
        name="pack",
    )(
        me,
        rr,
        x_input,
        z_input,
        dt_input,
        jnp.transpose(b_input, (0, 2, 1)),
        jnp.transpose(c_input, (0, 2, 1)),
        prefix_length.reshape(1, rows),
    )
    payload = [payload[0]] + [trade(payload[k], "dp", n, k) for k in range(1, n)]
    par = jnp.concatenate(
        [conv_weight, conv_bias[None], dt_bias[None], skip_gain[None], jnp.zeros((1, ch), F32)], 0
    )
    conv = jnp.transpose(conv_cache, (1, 0, 2))
    y_buf, kept = None, []
    for k in range(n):
        y_buf, st = ssm(
            k, n, per, steps, me, ss, payload[k], par, decay_rate, conv, state_cache, y_buf
        )
        kept.append(st)
    y_own = y_buf.reshape(n * steps * per, ch)
    ys = [y_own] + [trade(y_own, "dp", n, k) for k in range(1, n)]

    total_sel = 2 * m * n * (pe + rm)
    ids_t = route_ids.reshape(total, -1).T
    wts_t = route_weight.reshape(total, -1).T
    meta_at = 3 * steps * ch // 128
    sel, share, expand = pl.pallas_call(
        functools.partial(select_kernel, n, m, per, steps, rows, rm, pe, width),
        grid=(1,),
        in_specs=[sm, sm]
        + [pl.BlockSpec(ids_t.shape, lambda g: (0, 0))] * 2
        + [pl.BlockSpec((per, 128), lambda g: (0, meta_at))] * n,
        out_specs=[
            pl.BlockSpec((total_sel, total), lambda g: (0, 0)),
            pl.BlockSpec((cap, 128), lambda g: (0, 0)),
            pl.BlockSpec((cap, total), lambda g: (0, 0)),
        ],
        out_shape=[
            jax.ShapeDtypeStruct((total_sel, total), BF),
            jax.ShapeDtypeStruct((cap, 128), F32),
            jax.ShapeDtypeStruct((cap, total), BF),
        ],
        compiler_params=params(24),
        cost_estimate=cost(1e7, 1 << 20),
        name="select",
    )(me, expert_slots, ids_t, wts_t, *payload)

    counts = (m * n * pe, m * n * rm) * 2
    wb = wc // 4
    keep_slot, keep_own, send_slot_rows, send_own = pl.pallas_call(
        functools.partial(project_kernel, n, counts),
        grid=(wc // wb,),
        in_specs=[pl.BlockSpec(y_own.shape, lambda g: (0, 0))] * n
        + [
            pl.BlockSpec((total_sel, total), lambda g: (0, 0)),
            pl.BlockSpec((ch, wb), lambda g: (0, g)),
        ],
        out_specs=[pl.BlockSpec((count, wb), lambda g: (0, g)) for count in counts],
        out_shape=[jax.ShapeDtypeStruct((count, wc), BF) for count in counts],
        scratch_shapes=[pltpu.VMEM((total, ch), BF), pltpu.VMEM((total_sel, ch), BF)],
        compiler_params=params(40),
        cost_estimate=cost(5e9, 12 << 20),
        name="project",
    )(*ys, sel, out_weight)

    def reduce_rows(keep, send, each):
        both = keep.astype(F32) + trade(send, "core", 2, 1).astype(F32)
        both = both.reshape(m, n * each, wc)
        out = both[0]
        narrow = both.astype(BF)
        for k in range(1, m):
            out = out + trade(narrow[k], "z", m, k).astype(F32)
        out = out.astype(BF).reshape(n, each, wc)
        return [out[0]] + [trade(out[k], "dp", n, k) for k in range(1, n)]

    hid = reduce_rows(keep_slot, send_slot_rows, pe)
    wide = [h.astype(F32) for h in hid]
    square = sum(jnp.sum(h * h, axis=1, keepdims=True) for h in wide)
    scale = lax.rsqrt(square / dm + 1e-05)
    normed = jnp.concatenate(
        [
            (wide[k] * scale * lax.dynamic_slice_in_dim(norm_gain, (d ^ k) * wc, wc)[None]).astype(BF)
            for k in range(n)
        ],
        axis=1,
    )
    near = [normed] + [trade(normed, "z", m, k) for k in range(1, m)]
    xs = []
    for piece in near:
        xs += [piece, trade(piece, "core", 2, 1)]

    kb = min(512, wc)
    wide_k = wc // kb
    act = pl.pallas_call(
        functools.partial(gate_kernel, 2 * m),
        grid_spec=pltpu.PrefetchScalarGridSpec(
            num_scalar_prefetch=1,
            grid=(dm // kb,),
            in_specs=[pl.BlockSpec((pe, dm), lambda g, *_: (0, 0))] * (2 * m)
            + [pl.BlockSpec((cap, 128), lambda g, *_: (0, 0))]
            + [
                pl.BlockSpec(
                    (kb, width), lambda g, w: ((w[0] ^ (g // wide_k)) * wide_k + g % wide_k, 0)
                )
            ]
            * 2,
            out_specs=pl.BlockSpec((cap, width), lambda g, *_: (0, 0)),
            scratch_shapes=[
                pltpu.VMEM((cap, dm), BF),
                pltpu.VMEM((cap, width), F32),
                pltpu.VMEM((cap, width), F32),
            ],
        ),
        out_shape=jax.ShapeDtypeStruct((cap, width), BF),
        compiler_params=params(40),
        cost_estimate=cost(4 * cap * dm * width, 4 * dm * width),
        name="gate",
    )(me, *xs, share, gate_weight, up_weight)

    half = dm // 2
    pc = half // m

    def down(h):
        cb = min(pc, 1024)
        per_z = pc // cb
        return pl.pallas_call(
            down_kernel,
            grid_spec=pltpu.PrefetchScalarGridSpec(
                num_scalar_prefetch=1,
                grid=(half // cb,),
                in_specs=[
                    pl.BlockSpec((cap, width), lambda g, *_: (0, 0)),
                    pl.BlockSpec(
                        (width, cb),
                        lambda g, w: (
                            0,
                            ((w[2] ^ h) * m + (w[1] ^ (g // per_z))) * per_z + g % per_z,
                        ),
                    ),
                ],
                out_specs=pl.BlockSpec((cap, cb), lambda g, *_: (0, g)),
            ),
            out_shape=jax.ShapeDtypeStruct((cap, half), BF),
            compiler_params=params(32),
            cost_estimate=cost(2 * cap * half * width, 2 * half * width),
            name=f"down{h}",
        )(me, act, down_weight)

    far = trade(down(1), "core", 2, 1)
    both = down(0).astype(F32) + far.astype(F32)
    out = both[:, :pc]
    narrow = both.astype(BF)
    for k in range(1, m):
        out = out + trade(narrow[:, k * pc : (k + 1) * pc], "z", m, k).astype(F32)
    spread = lax.dot_general(expand, out.astype(BF), TN, preferred_element_type=F32).astype(BF)
    share_rows = total // n
    mine = lax.dynamic_slice_in_dim(spread, d * share_rows, share_rows, 0).astype(F32)
    for k in range(1, n):
        piece = lax.dynamic_slice_in_dim(spread, (d ^ k) * share_rows, share_rows, 0)
        mine = mine + trade(piece, "dp", n, k).astype(F32)
    mine = mine.astype(BF)
    parts = []
    for q in range(2 * m):
        at = ((zz ^ (q // 2)) * 2 + (cc ^ (q % 2))) * rm
        piece = lax.dynamic_slice_in_dim(mine, at, rm, 0)
        parts.append(piece if q == 0 else trade(piece, ("z", "core"), 2 * m, q))

    own = reduce_rows(keep_own, send_own, rm)
    mixed = pl.pallas_call(
        functools.partial(final_kernel, n, m),
        in_specs=[sm] + [vm] * (n + 2 * m),
        out_specs=vm,
        out_shape=jax.ShapeDtypeStruct((rm, dm), BF),
        scratch_shapes=[pltpu.VMEM((rm, dm), F32)],
        compiler_params=params(16),
        cost_estimate=cost(1e5, 1 << 19),
        name="final",
    )(me, *own, *parts)

    back = [kept[0]] + [trade(kept[k], "dp", n, k) for k in range(1, n)]
    new_state = None
    for k in range(n):
        new_state = place(k, n, per, rows, states, me, rr, back[k], new_state)
    low = kept[0].shape[0] - per * states
    tail_at = per * states // low
    new_tail = pl.pallas_call(
        functools.partial(tail_kernel, n, per, taps),
        grid=(1,),
        in_specs=[sm, sm, pl.BlockSpec(x_input.shape, lambda g: (0, 0, 0))]
        + [pl.BlockSpec((low, ch), lambda g: (tail_at, 0))] * n,
        out_specs=pl.BlockSpec((taps, rows, ch), lambda g: (0, 0, 0)),
        out_shape=jax.ShapeDtypeStruct((taps, rows, ch), F32),
        compiler_params=params(16),
        cost_estimate=cost(1e5, 1 << 20),
        name="tail",
    )(me, rr, x_input, *back)
    return (mixed, new_state, jnp.transpose(new_tail, (1, 0, 2)))


def solution(mesh):
    n = mesh.shape["dp"]
    m = mesh.shape["expert"] // 2
    split = Mesh(mesh.devices.reshape(n, m, 2), ("dp", "z", "core"))
    e = ("z", "core")
    de = ("dp", "z", "core")
    in_specs = (
        P("dp", None, e),
        P("dp", None, e),
        P(),
        P("dp", None, None),
        P("dp"),
        P(None, "dp", e),
        P(None, "dp", e),
        P(None, "dp", e),
        P(None, "dp", None),
        P(None, "dp", None),
        P(None, e),
        P(e),
        P(e),
        P(None, e),
        P(e),
        P(e, "dp"),
        P(),
        P(),
        P(),
        P(),
        P(None, de),
        P(None, de),
        P(de, None),
    )
    out_specs = (P(de, None), P("dp", None, e), P("dp", None, e))
    return jax.shard_map(body, mesh=split, in_specs=in_specs, out_specs=out_specs, check_vma=False)
```

```python
import functools

import jax
import jax.numpy as jnp
from jax import lax
from jax.experimental import pallas as pl
from jax.experimental.pallas import tpu as pltpu
from jax.sharding import Mesh
from jax.sharding import PartitionSpec as P

FFW = 12288
BF = jnp.bfloat16
F32 = jnp.float32
META = 256
TABLE = 96
PREFIX = 64
NT = (((1,), (1,)), ((), ()))
TN = (((0,), (0,)), ((), ()))


def cost(flops, moved):
    return pl.CostEstimate(flops=int(flops), bytes_accessed=int(moved), transcendentals=0)


def params(limit):
    return pltpu.CompilerParams(vmem_limit_bytes=limit << 20)


def iota(shape, dim):
    return lax.broadcasted_iota(jnp.int32, shape, dim)


def trade(piece, axis, size, k):
    return lax.ppermute(piece, axis, [(i, i ^ k) for i in range(size)])


def pack_kernel(n, per, me, rr, x, z, dt, b, c, prefix, *rest):
    outs, m_scr = rest[:n], rest[n]
    steps, rows, ch = x.shape
    states = b.shape[1]
    m_scr[...] = jnp.zeros_like(m_scr)
    for t in range(steps):
        m_scr[2 * t * states : (2 * t + 1) * states, :] = b[t]
        m_scr[(2 * t + 1) * states : (2 * t + 2) * states, :] = c[t]
    m_scr[PREFIX : PREFIX + 1, :] = prefix[...].astype(F32)
    rowcol = jnp.zeros((n * per, 1), jnp.int32)
    table = jnp.zeros((1, 128), F32)
    sub = iota((n * per, 1), 0)
    lane = iota((1, 128), 1)
    for k in range(n):
        for i in range(per):
            rowcol = jnp.where(sub == k * per + i, rr[0, me[0] ^ k, i], rowcol)
            q = k * per + i
            table = jnp.where(lane == TABLE + q, rr[0, k, i].astype(F32), table)
    hot = rowcol == iota((n * per, rows), 1)
    hot_b = hot.astype(BF)
    for a, src in enumerate((x, z, dt)):
        for t in range(steps):
            got = jnp.dot(hot_b, src[t], preferred_element_type=F32).astype(BF)
            at = (a * steps + t) * ch
            for k in range(n):
                outs[k][:, at : at + ch] = got[k * per : (k + 1) * per]
    meta = lax.dot_general(
        hot.astype(F32), m_scr[...], NT, precision=lax.Precision.HIGHEST, preferred_element_type=F32
    )
    meta = meta + table
    hi = meta.astype(BF)
    lo = (meta - hi.astype(F32)).astype(BF)
    at = 3 * steps * ch
    for k in range(n):
        outs[k][:, at : at + 128] = hi[k * per : (k + 1) * per]
        outs[k][:, at + 128 : at + 256] = lo[k * per : (k + 1) * per]


def ssm_kernel(first, groups, n, per, steps, me, ss, *refs):
    wide = 3 * steps + 1
    if first:
        refs = refs[1:]
    loads = refs[: groups * wide]
    par, decay, conv = refs[groups * wide : groups * wide + 3]
    rest = refs[groups * wide + 3 :]
    state, (y_out, *st_outs) = rest[:per], rest[per : per + 1 + groups]
    arrs, meta, y_scr, tail_scr, bc_scr = rest[per + 1 + groups :]
    group = pl.program_id(0)
    for q in range(groups):

        @pl.when(group == q)
        def _():
            for a in range(3 * steps):
                arrs[a] = loads[q * wide + a][...]
            meta[...] = loads[q * wide + wide - 1][...]

    taps = conv.shape[0]
    states, cb = decay.shape
    val = meta[:, :128].astype(F32) + meta[:, 128:].astype(F32)
    bc_scr[...] = jnp.transpose(jnp.concatenate([val, jnp.zeros((128 - per, 128), F32)], axis=0))
    src = me[0] ^ (group + first)
    for j in range(taps):
        for i in range(per):
            tail_scr[j, i : i + 1, :] = conv[j, pl.ds(ss[me[0], src, i], 1), :]
    prefix = val[:, PREFIX : PREFIX + 1]
    window = [
        tail_scr[j] * (prefix >= float(taps - j)).astype(F32) for j in range(taps)
    ]
    deltas, us, skips, gates = [], [], [], []
    for t in range(steps):
        window.append(arrs[t].astype(F32))
        acc = window[t] * par[0:1, :]
        for j in range(1, taps + 1):
            acc = acc + window[t + j] * par[j : j + 1, :]
        acc = acc + par[taps + 1 : taps + 2, :]
        xc = acc * jax.nn.sigmoid(acc)
        raw = arrs[2 * steps + t].astype(F32) + par[taps + 2 : taps + 3, :]
        delta = jnp.maximum(raw, 0.0) + jnp.log1p(jnp.exp(-jnp.abs(raw)))
        zt = arrs[steps + t].astype(F32)
        deltas.append(-delta)
        us.append(delta * xc)
        skips.append(par[taps + 3 : taps + 4, :] * xc)
        gates.append(zt * jax.nn.sigmoid(zt))
    dec = decay[...]
    low = st_outs[0].shape[0] - per * states
    kept = window[steps:taps]
    kept.append(jnp.zeros((low - per * len(kept), cb), F32))
    kept = jnp.concatenate(kept, axis=0)
    ends = []
    for i in range(per):
        st = state[i][0]
        for t in range(steps):
            at = 2 * t * states
            bcol = bc_scr[at : at + states, i : i + 1]
            ccol = bc_scr[at + states : at + 2 * states, i : i + 1]
            st = jnp.exp(deltas[t][i : i + 1] * dec) * st + us[t][i : i + 1] * bcol
            y_scr[t, i : i + 1, :] = jnp.sum(ccol * st, axis=0, keepdims=True)
        for q in range(groups):

            @pl.when(group == q)
            def _():
                st_outs[q][i * states : (i + 1) * states, :] = st.astype(st_outs[q].dtype)

    for q in range(groups):

        @pl.when(group == q)
        def _():
            st_outs[q][per * states :, :] = kept.astype(st_outs[q].dtype)

    for t in range(steps):
        out = (y_scr[t] + skips[t]) * gates[t]
        y_out[0, t * per : (t + 1) * per, :] = out.astype(BF)


def ssm(first, n, per, steps, me, ss, payloads, par, decay, conv, state, y_buf):
    groups = len(payloads)
    states, ch = decay.shape
    blocks = 2
    cb = ch // blocks
    taps = conv.shape[0]
    low = -(-(taps - steps) * per // 16) * 16

    def held(q, gk, g):
        return jnp.where(gk < q, 0, jnp.where(gk > q, blocks - 1, g))

    specs, args = [], []
    for q in range(groups):
        for a in range(3 * steps):
            specs.append(
                pl.BlockSpec(
                    (per, cb),
                    functools.partial(
                        lambda q, a, gk, g, *_: (0, a * blocks + held(q, gk, g)), q, a
                    ),
                )
            )
        specs.append(pl.BlockSpec((per, META), lambda gk, g, *_: (0, 3 * steps * ch // META)))
        args += [payloads[q]] * (3 * steps + 1)
    specs.append(pl.BlockSpec((par.shape[0], cb), lambda gk, g, *_: (0, g)))
    specs.append(pl.BlockSpec((states, cb), lambda gk, g, *_: (0, g)))
    specs.append(pl.BlockSpec((taps, conv.shape[1], cb), lambda gk, g, *_: (0, 0, g)))
    for i in range(per):
        specs.append(
            pl.BlockSpec(
                (1, states, cb),
                functools.partial(
                    lambda i, gk, g, m, s: (s[m[0], m[0] ^ (gk + first), i], 0, g), i
                ),
            )
        )
    args += [par, decay, conv] + [state] * per
    alias = {}
    if first:
        specs = [pl.BlockSpec(memory_space=pl.ANY)] + specs
        args = [y_buf] + args
        alias = {2: 0}
    st_type = BF if first else F32
    return pl.pallas_call(
        functools.partial(ssm_kernel, first, groups, n, per, steps),
        grid_spec=pltpu.PrefetchScalarGridSpec(
            num_scalar_prefetch=2,
            grid=(groups, blocks),
            in_specs=specs,
            out_specs=[pl.BlockSpec((1, steps * per, cb), lambda gk, g, *_: (gk + first, 0, g))]
            + [
                pl.BlockSpec(
                    (per * states + low, cb),
                    functools.partial(lambda q, gk, g, *_: (0, held(q, gk, g)), q),
                )
                for q in range(groups)
            ],
            scratch_shapes=[
                pltpu.VMEM((3 * steps, per, cb), BF),
                pltpu.VMEM((per, META), BF),
                pltpu.VMEM((steps, per, cb), F32),
                pltpu.VMEM((taps, per, cb), F32),
                pltpu.VMEM((128, 128), F32),
            ],
        ),
        out_shape=[jax.ShapeDtypeStruct((n, steps * per, ch), BF)]
        + [jax.ShapeDtypeStruct((per * states + low, ch), st_type)] * groups,
        input_output_aliases=alias,
        compiler_params=params(16),
        cost_estimate=cost(3e6 * groups, groups * 3 << 20),
        name=f"ssm{first}",
    )(me, ss, *args)


def select_kernel(n, m, per, steps, rows, rm, pe, width, me, es, ids, wts, *refs):
    tables = refs[:n]
    sel_slot, sel_own, share, expand = refs[n:]
    cores = m * 2
    d, zz, cc = me[0], me[1], me[2]
    total = steps * n * rows
    choices = ids.shape[0]
    sub8 = iota((8, total), 0)
    match = jnp.zeros((8, total), F32)
    own_share = jnp.zeros((1, total), F32)
    hits = []
    for kd in range(n):
        eid = es[((d ^ kd) * (cores * width)) // FFW]
        hit = jnp.zeros((1, total), F32)
        for q in range(choices):
            same = ids[q : q + 1, :] == eid
            hit = jnp.where(same, 1.0, hit)
            if kd == 0:
                own_share = own_share + jnp.where(same, wts[q : q + 1, :], 0.0)
        hits.append(hit)
        match = jnp.where(sub8 == kd, hit, match)
    before = (iota((total, total), 0) < iota((total, total), 1)).astype(BF)
    pos = jnp.dot(match.astype(BF), before, preferred_element_type=F32)
    pos = jnp.where(match > 0.0, pos, -1.0)
    col = iota((pe, 1), 0)
    parts, owns = [], []
    for h in range(2):
        for kz in range(m):
            first = ((zz ^ kz) * 2 + (cc ^ h)) * pe
            want = (col + first).astype(F32)
            for kd in range(n):
                parts.append((pos[kd : kd + 1, :] == want).astype(BF))
        row = iota((m * n * rm, 1), 0)
        kz_v = row // (n * rm)
        kd_v = (row // rm) % n
        true = ((d ^ kd_v) * cores + (zz ^ kz_v) * 2 + (cc ^ h)) * rm + row % rm
        owns.append((true == iota((m * n * rm, total), 1)).astype(BF))
    sel_true = jnp.concatenate(parts + owns, axis=0)
    j = iota((total, 1), 0)
    ko = j // (n * steps * per)
    kd = (j // (steps * per)) % n
    tab = jnp.zeros((8, 128), F32)
    for q in range(n):
        tab = jnp.where(iota((8, 128), 0) == q, tables[q][0:1, :].astype(F32), tab)
    pick = (iota((total, 8), 1) == (ko ^ kd)).astype(BF)
    tj = jnp.dot(pick, tab.astype(BF), preferred_element_type=F32)
    lane = TABLE + (d ^ ko) * per + j % per
    local = jnp.sum(jnp.where(iota((total, 128), 1) == lane, tj, 0.0), axis=1, keepdims=True)
    true = ((j // per) % steps) * (n * rows) + (d ^ ko ^ kd) * rows + local.astype(jnp.int32)
    perm = (true == iota((total, total), 1)).astype(BF)
    sel = lax.dot_general(sel_true, perm, NT, preferred_element_type=F32).astype(BF)
    count = sel_slot.shape[0]
    sel_slot[...] = sel[:count]
    sel_own[...] = sel[count:]
    hot = pos[0:1, :] == iota((cores * pe, 1), 0).astype(F32)
    expand[...] = hot.astype(BF)
    mine = jnp.sum(jnp.where(hot, own_share, 0.0), axis=1, keepdims=True)
    share[...] = jnp.broadcast_to(mine, share.shape)


def project_kernel(n, *refs):
    ys = refs[:n]
    sel, w = refs[n : n + 2]
    keep, send, y_all, y_sel = refs[-4:]
    size = ys[0].shape[0]
    for q in range(n):
        y_all[q * size : (q + 1) * size, :] = ys[q][...]
    y_sel[...] = jnp.dot(sel[...], y_all[...], preferred_element_type=F32).astype(BF)
    half = keep.shape[0]
    wb = min(512, w.shape[1])

    @pl.loop(0, w.shape[1] // wb)
    def _(g):
        at = pl.ds(pl.multiple_of(g * wb, wb), wb)
        out = jnp.dot(y_sel[...], w[:, at], preferred_element_type=F32).astype(BF)
        keep[:, at] = out[:half]
        send[:, at] = out[half:]


def project(n, ys, sel, w, name, dep):
    vm = pl.BlockSpec(memory_space=pltpu.VMEM)
    count, total = sel.shape
    ch, wc = w.shape
    return pl.pallas_call(
        functools.partial(project_kernel, n),
        in_specs=[vm] * (n + 2) + [pl.BlockSpec(memory_space=pl.ANY)],
        out_specs=[vm] * 2,
        out_shape=[jax.ShapeDtypeStruct((count // 2, wc), BF)] * 2,
        scratch_shapes=[pltpu.VMEM((total, ch), BF), pltpu.VMEM((count, ch), BF)],
        compiler_params=params(8),
        cost_estimate=cost(2 * count * ch * wc, 2 * ch * wc),
        name=name,
    )(*ys, sel, w, dep)


def load_kernel(chunks, w, *refs):
    out, token, sem = refs[-3:]
    token[...] = jnp.zeros_like(token)
    size = w.shape[0] // chunks
    copies = [
        pltpu.make_async_copy(
            w.at[pl.ds(q * size, size)], out.at[pl.ds(q * size, size)], sem.at[q]
        )
        for q in range(chunks)
    ]
    for copy in copies:
        copy.start()
    for copy in copies:
        copy.wait()


def gate_kernel(m, me, *refs):
    pieces = 2 * m
    xs = refs[:pieces]
    share, gw, uw, act, x_scr, ubuf, usem = refs[pieces:]
    pe = xs[0].shape[0]
    ub, deep = ubuf.shape[2], ubuf.shape[0]
    nu = gw.shape[1] // ub

    def up_copy(j):
        return pltpu.make_async_copy(
            uw.at[:, pl.ds(pl.multiple_of(j * ub, ub), ub)],
            ubuf.at[lax.rem(j, deep)],
            usem.at[lax.rem(j, deep)],
        )

    for j in range(min(deep, nu)):
        up_copy(j).start()
    first = me[2] == 0
    for kz in range(m):
        own, other = xs[2 * kz][...].astype(F32), xs[2 * kz + 1][...].astype(F32)
        pair = jnp.concatenate(
            [jnp.where(first, own, other), jnp.where(first, other, own)], axis=0
        ).astype(BF)
        at = pl.multiple_of((me[1] ^ kz) * (2 * pe), 2 * pe)
        x_scr[pl.ds(at, 2 * pe), :] = pair

    @pl.loop(0, nu)
    def _(j):
        at = pl.ds(pl.multiple_of(j * ub, ub), ub)
        gated = jnp.dot(x_scr[...], gw[:, at], preferred_element_type=F32)
        up_copy(j).wait()
        upped = jnp.dot(x_scr[...], ubuf[lax.rem(j, deep)], preferred_element_type=F32)

        @pl.when(j + deep < nu)
        def _():
            up_copy(j + deep).start()

        act[:, at] = (gated * jax.nn.sigmoid(gated) * upped * share[:, 0:1]).astype(BF)


def down_kernel(m, deps, me, act, dw, *refs):
    send, keep, dbuf, dsem = refs[deps:]
    pc, deep = dbuf.shape[2], dbuf.shape[0]
    nd = 2 * m

    def down_copy(i):
        h = jnp.where(i < m, 1, 0)
        block = (me[2] ^ h) * m + (me[1] ^ lax.rem(i, m))
        return pltpu.make_async_copy(
            dw.at[:, pl.ds(pl.multiple_of(block * pc, pc), pc)],
            dbuf.at[lax.rem(i, deep)],
            dsem.at[lax.rem(i, deep)],
        )

    for i in range(min(deep, nd)):
        down_copy(i).start()

    @pl.loop(0, nd)
    def _(i):
        down_copy(i).wait()
        out = jnp.dot(act[...], dbuf[lax.rem(i, deep)], preferred_element_type=F32).astype(BF)
        at = pl.ds(pl.multiple_of(lax.rem(i, m) * pc, pc), pc)

        @pl.when(i < m)
        def _():
            send[:, at] = out

        @pl.when(i >= m)
        def _():
            keep[:, at] = out

        @pl.when(i + deep < nd)
        def _():
            down_copy(i + deep).start()


def pair_rows_kernel(count, keep, got, *refs):
    outs = refs[-count:]
    size = outs[0].shape[0]
    for k in range(count):
        at = slice(k * size, (k + 1) * size)
        both = keep[at].astype(F32) + got[at].astype(F32)
        outs[k][...] = both.astype(outs[k].dtype)


def pair_cols_kernel(count, keep, got, *refs):
    outs = refs[-count:]
    size = outs[0].shape[1]
    for k in range(count):
        at = slice(k * size, (k + 1) * size)
        both = keep[:, at].astype(F32) + got[:, at].astype(F32)
        outs[k][...] = both.astype(outs[k].dtype)


def sum_rows_kernel(count, parts, *refs):
    outs = refs[-parts:]
    size = outs[0].shape[0]
    total = refs[0][...]
    for k in range(1, count):
        total = total + refs[k][...].astype(F32)
    for k in range(parts):
        outs[k][...] = total[k * size : (k + 1) * size].astype(BF)


def norm_kernel(n, me, gain, *refs):
    hid, out = refs[:n], refs[n]
    wc = hid[0].shape[1]
    wide = [h[...].astype(F32) for h in hid]
    square = sum(jnp.sum(h * h, axis=1, keepdims=True) for h in wide)
    scale = lax.rsqrt(square / (n * wc) + 1e-05)
    for k in range(n):
        at = pl.ds(pl.multiple_of((me[0] ^ k) * wc, wc), wc)
        out[:, at] = (wide[k] * scale * gain[:, at]).astype(BF)


def spread_kernel(n, m, me, expand, *refs):
    outs, scr = refs[-n - 1 : -1], refs[-1]
    out = refs[0][...]
    for k in range(1, m):
        out = out + refs[k][...].astype(F32)
    scr[...] = lax.dot_general(expand[...], out.astype(BF), TN, preferred_element_type=F32)
    size = outs[0].shape[0]
    for k in range(n):
        got = scr[pl.ds(pl.multiple_of((me[0] ^ k) * size, size), size), :]
        outs[k][...] = got.astype(outs[k].dtype)


def deal_kernel(n, m, me, *refs):
    keep, send, scr = refs[n:]
    total = refs[0][...]
    for k in range(1, n):
        total = total + refs[k][...].astype(F32)
    scr[...] = total
    rm = keep.shape[0] // m
    for q in range(2 * m):
        block = (me[1] ^ (q // 2)) * 2 + (me[2] ^ (q % 2))
        out = send if q % 2 else keep
        if rm % 8 == 0:
            got = scr[pl.ds(pl.multiple_of(block * rm, rm), rm), :]
        else:
            got = scr[:rm]
            for b in range(1, 2 * m):
                got = jnp.where(block == b, scr[b * rm : (b + 1) * rm], got)
        out[(q // 2) * rm : (q // 2 + 1) * rm, :] = got.astype(BF)


def pair_kernel(m, keep, got, *outs):
    rm = outs[0].shape[0]
    pc = keep.shape[1]
    for k in range(m):
        outs[k][:, :pc] = keep[k * rm : (k + 1) * rm]
        outs[k][:, pc:] = got[k * rm : (k + 1) * rm]


def hold_kernel(*refs):
    pass


def small(kern, name, outs, args, deps=(), scr=()):
    vm = pl.BlockSpec(memory_space=pltpu.VMEM)
    sm = pl.BlockSpec(memory_space=pltpu.SMEM)
    count = len(args)

    def run(*refs):
        kern(*refs[:count], *refs[count + len(deps) :])

    specs = [sm if a.dtype == jnp.int32 and a.ndim == 1 else vm for a in args]
    return pl.pallas_call(
        run,
        in_specs=specs + [pl.BlockSpec(memory_space=pl.ANY)] * len(deps),
        out_specs=[vm] * len(outs),
        out_shape=[jax.ShapeDtypeStruct(*o) for o in outs],
        scratch_shapes=list(scr),
        compiler_params=params(8),
        cost_estimate=cost(1e6, 1 << 20),
        name=name,
    )(*args, *deps)


def place_kernel(n, states, me, rr, *refs):
    srcs, (out, token, buf, sem) = refs[:n], refs[-4:]
    token[...] = jnp.zeros_like(token)
    i, last = pl.program_id(0), pl.num_programs(0) - 1
    slot = lax.rem(i, 2)

    def copies(step, where):
        return [
            pltpu.make_async_copy(buf.at[where, k], out.at[rr[0, me[0] ^ k, step]], sem.at[where, k])
            for k in range(n)
        ]

    @pl.when(i >= 2)
    def _():
        for copy in copies(i - 2, slot):
            copy.wait()

    for k in range(n):
        buf[slot, k] = srcs[k][...].astype(F32)
    for copy in copies(i, slot):
        copy.start()

    @pl.when(i == last)
    def _():
        for copy in copies(i - 1, 1 - slot):
            copy.wait()
        for copy in copies(i, slot):
            copy.wait()


def place(n, per, rows, states, me, rr, srcs, dep):
    ch = srcs[0].shape[1]
    return pl.pallas_call(
        functools.partial(place_kernel, n, states),
        grid_spec=pltpu.PrefetchScalarGridSpec(
            num_scalar_prefetch=2,
            grid=(per,),
            in_specs=[pl.BlockSpec((states, ch), lambda i, *_: (i, 0))] * n
            + [pl.BlockSpec(memory_space=pl.ANY)],
            out_specs=[
                pl.BlockSpec(memory_space=pl.ANY),
                pl.BlockSpec((8, 128), lambda i, *_: (0, 0)),
            ],
            scratch_shapes=[
                pltpu.VMEM((2, n, states, ch), F32),
                pltpu.SemaphoreType.DMA((2, n)),
            ],
        ),
        out_shape=[
            jax.ShapeDtypeStruct((rows, states, ch), F32),
            jax.ShapeDtypeStruct((8, 128), F32),
        ],
        compiler_params=params(8),
        cost_estimate=cost(1e5, 8 << 20),
        name="place",
    )(me, rr, *srcs, dep)


def tail_kernel(n, per, taps, me, rr, x, *refs):
    tails, (out, token) = refs[:n], refs[-2:]
    token[...] = jnp.zeros_like(token)
    steps = x.shape[0]
    keep = taps - steps
    for t in range(steps):
        out[keep + t] = x[t].astype(F32)
    for k in range(n):
        block = tails[k][...].astype(F32)
        for j in range(keep):
            for i in range(per):
                q = j * per + i
                out[j, pl.ds(rr[0, me[0] ^ k, i], 1), :] = block[q : q + 1, :]


def final_kernel(n, m, me, *refs):
    hid = refs[:n]
    parts = refs[n : n + m]
    out, acc = refs[-2:]
    wc = hid[0].shape[1]
    for k in range(n):
        acc[:, pl.ds(pl.multiple_of((me[0] ^ k) * wc, wc), wc)] = hid[k][...].astype(F32)
    pc = parts[0].shape[1] // 2
    for q in range(2 * m):
        zs, h = me[1] ^ (q // 2), q % 2
        where = pl.ds(pl.multiple_of(((me[2] ^ h) * m + zs) * pc, pc), pc)
        got = parts[q // 2][:, h * pc : (h + 1) * pc].astype(F32)
        acc[:, where] = acc[:, where] + got
    out[...] = acc[...].astype(BF)


def body(
    conv_cache,
    state_cache,
    send_slot,
    recv_row,
    prefix_length,
    x_input,
    z_input,
    dt_input,
    b_input,
    c_input,
    conv_weight,
    conv_bias,
    dt_bias,
    decay_rate,
    skip_gain,
    out_weight,
    norm_gain,
    route_ids,
    route_weight,
    expert_slots,
    gate_weight,
    up_weight,
    down_weight,
):
    n = lax.axis_size("dp")
    m = lax.axis_size("z")
    d, zz, cc = lax.axis_index("dp"), lax.axis_index("z"), lax.axis_index("core")
    me = jnp.stack([d, zz, cc]).astype(jnp.int32)
    steps, rows, ch = x_input.shape
    per = rows // n
    taps = conv_cache.shape[1]
    states = state_cache.shape[1]
    total = steps * n * rows
    cap = total // 4
    pe = cap // (2 * m)
    rm = total // (n * 2 * m)
    width = gate_weight.shape[1]
    wc = out_weight.shape[1]
    dm = n * wc
    rr, ss = recv_row, send_slot
    vm = pl.BlockSpec(memory_space=pltpu.VMEM)
    sm = pl.BlockSpec(memory_space=pltpu.SMEM)

    in_hbm = functools.partial(pltpu.with_memory_space_constraint, memory_space=pltpu.HBM)

    def whole(a):
        return pl.BlockSpec(a.shape, lambda g: (0,) * a.ndim)

    src = (
        x_input,
        z_input,
        dt_input,
        jnp.transpose(b_input, (0, 2, 1)),
        jnp.transpose(c_input, (0, 2, 1)),
        prefix_length.reshape(1, rows),
    )
    src = [in_hbm(a) for a in src]
    packed = jax.ShapeDtypeStruct((per, 3 * steps * ch + META), BF)
    payload = pl.pallas_call(
        functools.partial(pack_kernel, n, per),
        grid=(1,),
        in_specs=[sm, sm] + [whole(a) for a in src],
        out_specs=[whole(packed)] * n,
        out_shape=[packed] * n,
        scratch_shapes=[pltpu.VMEM((128, rows), F32)],
        compiler_params=params(12),
        cost_estimate=cost(1e6, 2 << 20),
        name="pack",
    )(me, recv_row, *src)
    payload = [payload[0]] + [trade(payload[k], "dp", n, k) for k in range(1, n)]
    par = jnp.concatenate(
        [conv_weight, conv_bias[None], dt_bias[None], skip_gain[None], jnp.zeros((1, ch), F32)], 0
    )
    conv = jnp.transpose(conv_cache, (1, 0, 2))
    fixed = (par, decay_rate, conv, in_hbm(state_cache))
    y_buf, own_kept = ssm(0, n, per, steps, me, ss, payload[:1], *fixed, None)
    y_buf, *kept = ssm(1, n, per, steps, me, ss, payload[1:], *fixed, y_buf)
    kept = [own_kept] + kept
    y_own = y_buf.reshape(n * steps * per, ch)
    ys = [y_own] + [trade(y_own, "dp", n, k) for k in range(1, n)]

    n_slot, n_own = 2 * m * n * pe, 2 * m * n * rm
    ids_t = route_ids.reshape(total, -1).T
    wts_t = route_weight.reshape(total, -1).T
    meta_at = 3 * steps * ch // 128
    sel_slot, sel_own, share, expand = pl.pallas_call(
        functools.partial(select_kernel, n, m, per, steps, rows, rm, pe, width),
        grid=(1,),
        in_specs=[sm, sm]
        + [pl.BlockSpec(ids_t.shape, lambda g: (0, 0))] * 2
        + [pl.BlockSpec((per, 128), lambda g: (0, meta_at))] * n,
        out_specs=[
            pl.BlockSpec((n_slot, total), lambda g: (0, 0)),
            pl.BlockSpec((n_own, total), lambda g: (0, 0)),
            pl.BlockSpec((cap, 128), lambda g: (0, 0)),
            pl.BlockSpec((cap, total), lambda g: (0, 0)),
        ],
        out_shape=[
            jax.ShapeDtypeStruct((n_slot, total), BF),
            jax.ShapeDtypeStruct((n_own, total), BF),
            jax.ShapeDtypeStruct((cap, 128), F32),
            jax.ShapeDtypeStruct((cap, total), BF),
        ],
        compiler_params=params(10),
        cost_estimate=cost(1e7, 1 << 20),
        name="select",
    )(me, expert_slots, ids_t, wts_t, *payload)

    width = gate_weight.shape[1]
    chunks = 8
    gate_here, loaded = pl.pallas_call(
        functools.partial(load_kernel, chunks),
        in_specs=[pl.BlockSpec(memory_space=pltpu.HBM), pl.BlockSpec(memory_space=pl.ANY)],
        out_specs=[vm, vm],
        out_shape=[pltpu.VMEM(gate_weight.shape, BF), jax.ShapeDtypeStruct((8, 128), F32)],
        scratch_shapes=[pltpu.SemaphoreType.DMA((chunks,))],
        compiler_params=params(1),
        cost_estimate=cost(0, 4 * gate_weight.size),
        name="load",
    )(in_hbm(gate_weight), y_own)
    anyspace = pl.BlockSpec(memory_space=pl.ANY)

    def add_core(keep, send, each, name, dep=()):
        got = trade(send, "core", 2, 1)
        shape = (n * each, wc)
        outs = [(shape, F32)] + [(shape, BF)] * (m - 1)
        return small(functools.partial(pair_rows_kernel, m), name, outs, (keep, got), dep)

    def send_z(parts):
        return [parts[0]] + [trade(parts[k], "z", m, k) for k in range(1, m)]

    def add_z(got, each, name, dep=()):
        outs = [((each, wc), BF)] * n
        out = small(functools.partial(sum_rows_kernel, m, n), name, outs, got, dep)
        return [out[0]] + [trade(out[k], "dp", n, k) for k in range(1, n)]

    keep_slot, send_slot_rows = project(n, ys, sel_slot, out_weight, "project_slot", loaded)
    parts = add_core(keep_slot, send_slot_rows, pe, "core_slot")
    slot_z = send_z(parts)
    keep_own, send_own = project(n, ys, sel_own, out_weight, "project_own", slot_z[1])
    hid = add_z(slot_z, pe, "z_slot", (keep_own,))
    [normed] = small(
        functools.partial(norm_kernel, n),
        "norm",
        [((pe, dm), BF)],
        (me, norm_gain.reshape(1, dm), *hid),
    )
    near = [normed] + [trade(normed, "z", m, k) for k in range(1, m)]
    xs = []
    for piece in near:
        xs += [piece, trade(piece, "core", 2, 1)]
    own_parts = add_core(keep_own, send_own, rm, "core_own", (near[1],))
    held = pl.pallas_call(
        hold_kernel,
        in_specs=[anyspace] * n,
        out_specs=[anyspace] * (n - 1),
        out_shape=[jax.ShapeDtypeStruct(k.shape, k.dtype) for k in kept[1:]],
        input_output_aliases={k: k for k in range(n - 1)},
        compiler_params=params(1),
        name="hold",
    )(*kept[1:], normed)
    back = [kept[0]] + [trade(held[k - 1], "dp", n, k) for k in range(1, n)]

    half = dm // 2
    pc = half // m
    ub = 256 if width % 256 == 0 else 128
    act = pl.pallas_call(
        functools.partial(gate_kernel, m),
        in_specs=[sm] + [vm] * (2 * m + 2) + [pl.BlockSpec(memory_space=pltpu.HBM)],
        out_specs=vm,
        out_shape=jax.ShapeDtypeStruct((cap, width), BF),
        scratch_shapes=[
            pltpu.VMEM((cap, dm), BF),
            pltpu.VMEM((2, dm, ub), BF),
            pltpu.SemaphoreType.DMA((2,)),
        ],
        compiler_params=params(14),
        cost_estimate=cost(4 * cap * dm * width, 4 * dm * width),
        name="gate",
    )(me, *xs, share, gate_here, in_hbm(up_weight))
    own_z = send_z(own_parts)
    own = add_z(own_z, rm, "z_own", (act,))
    deps = own_z[1:] + back[1:]
    send, keep = pl.pallas_call(
        functools.partial(down_kernel, m, len(deps)),
        in_specs=[sm, vm, pl.BlockSpec(memory_space=pltpu.HBM)] + [anyspace] * len(deps),
        out_specs=[vm] * 2,
        out_shape=[jax.ShapeDtypeStruct((cap, half), BF)] * 2,
        scratch_shapes=[pltpu.VMEM((3, width, pc), BF), pltpu.SemaphoreType.DMA((3,))],
        compiler_params=params(14),
        cost_estimate=cost(2 * cap * dm * width, 2 * dm * width),
        name="down",
    )(me, act, in_hbm(down_weight), *deps)

    got = trade(send, "core", 2, 1)
    outs = [((cap, pc), F32)] + [((cap, pc), BF)] * (m - 1)
    cols = small(functools.partial(pair_cols_kernel, m), "core_out", outs, (keep, got))
    moved = [cols[0]] + [trade(cols[k], "z", m, k) for k in range(1, m)]

    new_state, placed = place(n, per, rows, states, me, rr, back, cols[1])
    low = kept[0].shape[0] - per * states
    tail_at = per * states // low
    new_tail, placed = pl.pallas_call(
        functools.partial(tail_kernel, n, per, taps),
        grid=(1,),
        in_specs=[sm, sm, pl.BlockSpec(x_input.shape, lambda g: (0, 0, 0))]
        + [pl.BlockSpec((low, ch), lambda g: (tail_at, 0))] * n
        + [anyspace],
        out_specs=[
            pl.BlockSpec((taps, rows, ch), lambda g: (0, 0, 0)),
            pl.BlockSpec((8, 128), lambda g: (0, 0)),
        ],
        out_shape=[
            jax.ShapeDtypeStruct((taps, rows, ch), F32),
            jax.ShapeDtypeStruct((8, 128), F32),
        ],
        compiler_params=params(16),
        cost_estimate=cost(1e5, 1 << 20),
        name="tail",
    )(me, rr, x_input, *back, placed)

    share_rows = total // n
    outs = [((share_rows, pc), F32)] + [((share_rows, pc), BF)] * (n - 1)
    rows_out = small(
        functools.partial(spread_kernel, n, m),
        "spread",
        outs,
        (me, expand, *moved),
        (placed,),
        [pltpu.VMEM((total, pc), F32)],
    )
    mine = [rows_out[0]] + [trade(rows_out[k], "dp", n, k) for k in range(1, n)]
    deal_keep, deal_send = small(
        functools.partial(deal_kernel, n, m),
        "deal",
        [((m * rm, pc), BF)] * 2,
        (me, *mine),
        (),
        [pltpu.VMEM((share_rows, pc), F32)],
    )
    pieces = small(
        functools.partial(pair_kernel, m),
        "pair",
        [((rm, 2 * pc), BF)] * m,
        (deal_keep, trade(deal_send, "core", 2, 1)),
    )
    pieces = send_z(pieces)
    [mixed] = small(
        functools.partial(final_kernel, n, m),
        "final",
        [((rm, dm), BF)],
        (me, *own, *pieces),
        (),
        [pltpu.VMEM((rm, dm), F32)],
    )
    return (mixed, new_state, jnp.transpose(new_tail, (1, 0, 2)))


def solution(mesh):
    n = mesh.shape["dp"]
    m = mesh.shape["expert"] // 2
    split = Mesh(mesh.devices.reshape(n, m, 2), ("dp", "z", "core"))
    e = ("z", "core")
    de = ("dp", "z", "core")
    in_specs = (
        P("dp", None, e),
        P("dp", None, e),
        P(),
        P("dp", None, None),
        P("dp"),
        P(None, "dp", e),
        P(None, "dp", e),
        P(None, "dp", e),
        P(None, "dp", None),
        P(None, "dp", None),
        P(None, e),
        P(e),
        P(e),
        P(None, e),
        P(e),
        P(e, "dp"),
        P(),
        P(),
        P(),
        P(),
        P(None, de),
        P(None, de),
        P(de, None),
    )
    out_specs = (P(de, None), P("dp", None, e), P("dp", None, e))
    return jax.shard_map(body, mesh=split, in_specs=in_specs, out_specs=out_specs, check_vma=False)
```

```python
import functools

import jax
import jax.numpy as jnp
from jax import lax
from jax.experimental import pallas as pl
from jax.experimental.pallas import tpu as pltpu
from jax.sharding import Mesh
from jax.sharding import PartitionSpec as P

FFW = 12288
BF = jnp.bfloat16
F32 = jnp.float32
META = 256
TABLE = 96
PREFIX = 64
NT = (((1,), (1,)), ((), ()))
TN = (((0,), (0,)), ((), ()))


def cost(flops, moved):
    return pl.CostEstimate(flops=int(flops), bytes_accessed=int(moved), transcendentals=0)


def params(limit):
    return pltpu.CompilerParams(vmem_limit_bytes=limit << 20)


def iota(shape, dim):
    return lax.broadcasted_iota(jnp.int32, shape, dim)


def trade(piece, axis, size, k):
    return lax.ppermute(piece, axis, [(i, i ^ k) for i in range(size)])


def pack_kernel(n, per, me, rr, x, z, dt, b, c, prefix, *rest):
    outs, m_scr = rest[:n], rest[n]
    steps, rows, ch = x.shape
    states = b.shape[1]
    m_scr[...] = jnp.zeros_like(m_scr)
    for t in range(steps):
        m_scr[2 * t * states : (2 * t + 1) * states, :] = b[t]
        m_scr[(2 * t + 1) * states : (2 * t + 2) * states, :] = c[t]
    m_scr[PREFIX : PREFIX + 1, :] = prefix[...].astype(F32)
    rowcol = jnp.zeros((n * per, 1), jnp.int32)
    table = jnp.zeros((1, 128), F32)
    sub = iota((n * per, 1), 0)
    lane = iota((1, 128), 1)
    for k in range(n):
        for i in range(per):
            rowcol = jnp.where(sub == k * per + i, rr[0, me[0] ^ k, i], rowcol)
            q = k * per + i
            table = jnp.where(lane == TABLE + q, rr[0, k, i].astype(F32), table)
    hot = rowcol == iota((n * per, rows), 1)
    hot_b = hot.astype(BF)
    for a, src in enumerate((x, z, dt)):
        for t in range(steps):
            got = jnp.dot(hot_b, src[t], preferred_element_type=F32).astype(BF)
            at = (a * steps + t) * ch
            for k in range(n):
                outs[k][:, at : at + ch] = got[k * per : (k + 1) * per]
    meta = lax.dot_general(
        hot.astype(F32), m_scr[...], NT, precision=lax.Precision.HIGHEST, preferred_element_type=F32
    )
    meta = meta + table
    hi = meta.astype(BF)
    lo = (meta - hi.astype(F32)).astype(BF)
    at = 3 * steps * ch
    for k in range(n):
        outs[k][:, at : at + 128] = hi[k * per : (k + 1) * per]
        outs[k][:, at + 128 : at + 256] = lo[k * per : (k + 1) * per]


def ssm_kernel(groups, per, steps, me, ss, *refs):
    loads = refs[:groups]
    par, decay, conv, state, y_out = refs[groups : groups + 5]
    st_outs = refs[groups + 5 : 2 * groups + 5]
    y_scr, tail_scr, bc_scr, du_scr = refs[2 * groups + 5 :]
    taps, _, ch = conv.shape
    states = decay.shape[0]
    cb = y_scr.shape[2]
    lb = min(256, cb)
    low = st_outs[0].shape[0] - per * states
    at = 3 * steps * ch
    masks = []
    for q in range(groups):
        val = loads[q][:, at : at + 128].astype(F32) + loads[q][:, at + 128 : at + 256].astype(F32)
        full = jnp.concatenate([val, jnp.zeros((128 - per, 128), F32)], axis=0)
        bc_scr[q] = jnp.transpose(full)
        prefix = val[:, PREFIX : PREFIX + 1]
        masks.append([(prefix >= float(taps - j)).astype(F32) for j in range(taps)])

    @pl.loop(0, ch // cb)
    def _(g):
        base = pl.multiple_of(g * cb, cb)
        wide = pl.ds(base, cb)
        for q in range(groups):
            slots = [ss[me[0], me[0] ^ q, i] for i in range(per)]

            def load(a):
                return loads[q][:, pl.ds(pl.multiple_of(a * ch + base, cb), cb)].astype(F32)

            for j in range(taps):
                for i in range(per):
                    tail_scr[j, i : i + 1, :] = conv[j, pl.ds(slots[i], 1), wide]
            window = [tail_scr[j] * masks[q][j] for j in range(taps)]
            skips, gates = [], []
            for t in range(steps):
                window.append(load(t))
                acc = window[t] * par[0:1, wide]
                for j in range(1, taps + 1):
                    acc = acc + window[t + j] * par[j : j + 1, wide]
                acc = acc + par[taps + 1 : taps + 2, wide]
                xc = acc * jax.nn.sigmoid(acc)
                raw = load(2 * steps + t) + par[taps + 2 : taps + 3, wide]
                delta = jnp.maximum(raw, 0.0) + jnp.log1p(jnp.exp(-jnp.abs(raw)))
                zt = load(steps + t)
                du_scr[2 * t] = delta * -1.4426950408889634
                du_scr[2 * t + 1] = delta * xc
                skips.append(par[taps + 3 : taps + 4, wide] * xc)
                gates.append(zt * jax.nn.sigmoid(zt))
            kept = window[steps:taps]
            kept.append(jnp.zeros((low - per * len(kept), cb), F32))
            kept = jnp.concatenate(kept, axis=0)
            st_outs[q][per * states :, wide] = kept.astype(st_outs[q].dtype)
            for i in range(per):
                cols = []
                for k in range(2 * steps):
                    col = bc_scr[q, k * states : (k + 1) * states, i : i + 1]
                    cols.append(jnp.broadcast_to(col, (states, lb)))
                for l in range(cb // lb):
                    here = slice(l * lb, (l + 1) * lb)
                    there = pl.ds(pl.multiple_of(base + l * lb, lb), lb)
                    st = state[slots[i], :, there]
                    for t in range(steps):
                        dl = du_scr[2 * t, i : i + 1, here]
                        ul = du_scr[2 * t + 1, i : i + 1, here]
                        st = jnp.exp2(dl * decay[:, there]) * st + ul * cols[2 * t]
                        y_scr[t, i : i + 1, here] = jnp.sum(
                            cols[2 * t + 1] * st, axis=0, keepdims=True
                        )
                    st_outs[q][i * states : (i + 1) * states, there] = st.astype(st_outs[q].dtype)
            for t in range(steps):
                row = (q * steps + t) * per
                y_out[row : row + per, wide] = ((y_scr[t] + skips[t]) * gates[t]).astype(BF)


def ssm(per, steps, me, ss, payloads, par, decay, conv, state):
    groups = len(payloads)
    states, ch = decay.shape
    cb = ch // 4
    taps = conv.shape[0]
    low = -(-(taps - steps) * per // 16) * 16
    vm = pl.BlockSpec(memory_space=pltpu.VMEM)
    sm = pl.BlockSpec(memory_space=pltpu.SMEM)
    args = list(payloads) + [par, decay, conv, state]
    return pl.pallas_call(
        functools.partial(ssm_kernel, groups, per, steps),
        in_specs=[sm, sm] + [vm] * len(args),
        out_specs=[vm] * (1 + groups),
        out_shape=[jax.ShapeDtypeStruct((groups * steps * per, ch), BF)]
        + [
            jax.ShapeDtypeStruct((per * states + low, ch), BF if q else F32)
            for q in range(groups)
        ],
        scratch_shapes=[
            pltpu.VMEM((steps, per, cb), F32),
            pltpu.VMEM((taps, per, cb), F32),
            pltpu.VMEM((groups, 128, 128), F32),
            pltpu.VMEM((2 * steps, per, cb), F32),
        ],
        compiler_params=params(4),
        cost_estimate=cost(3e6 * groups, groups * 3 << 20),
        name="ssm",
    )(me, ss, *args)


def select_kernel(n, m, per, steps, rows, rm, pe, width, me, es, ids, wts, *refs):
    tables = refs[:n]
    sel_slot, sel_own, share, expand = refs[n:]
    cores = m * 2
    d, zz, cc = me[0], me[1], me[2]
    total = steps * n * rows
    choices = ids.shape[0]
    sub8 = iota((8, total), 0)
    match = jnp.zeros((8, total), F32)
    own_share = jnp.zeros((1, total), F32)
    hits = []
    for kd in range(n):
        eid = es[((d ^ kd) * (cores * width)) // FFW]
        hit = jnp.zeros((1, total), F32)
        for q in range(choices):
            same = ids[q : q + 1, :] == eid
            hit = jnp.where(same, 1.0, hit)
            if kd == 0:
                own_share = own_share + jnp.where(same, wts[q : q + 1, :], 0.0)
        hits.append(hit)
        match = jnp.where(sub8 == kd, hit, match)
    before = (iota((total, total), 0) < iota((total, total), 1)).astype(BF)
    pos = jnp.dot(match.astype(BF), before, preferred_element_type=F32)
    pos = jnp.where(match > 0.0, pos, -1.0)
    col = iota((pe, 1), 0)
    parts, owns = [], []
    for h in range(2):
        for kz in range(m):
            first = ((zz ^ kz) * 2 + (cc ^ h)) * pe
            want = (col + first).astype(F32)
            for kd in range(n):
                parts.append((pos[kd : kd + 1, :] == want).astype(BF))
        row = iota((m * n * rm, 1), 0)
        kz_v = row // (n * rm)
        kd_v = (row // rm) % n
        true = ((d ^ kd_v) * cores + (zz ^ kz_v) * 2 + (cc ^ h)) * rm + row % rm
        owns.append((true == iota((m * n * rm, total), 1)).astype(BF))
    sel_true = jnp.concatenate(parts + owns, axis=0)
    j = iota((total, 1), 0)
    ko = j // (n * steps * per)
    kd = (j // (steps * per)) % n
    tab = jnp.zeros((8, 128), F32)
    for q in range(n):
        tab = jnp.where(iota((8, 128), 0) == q, tables[q][0:1, :].astype(F32), tab)
    pick = (iota((total, 8), 1) == (ko ^ kd)).astype(BF)
    tj = jnp.dot(pick, tab.astype(BF), preferred_element_type=F32)
    lane = TABLE + (d ^ ko) * per + j % per
    local = jnp.sum(jnp.where(iota((total, 128), 1) == lane, tj, 0.0), axis=1, keepdims=True)
    true = ((j // per) % steps) * (n * rows) + (d ^ ko ^ kd) * rows + local.astype(jnp.int32)
    perm = (true == iota((total, total), 1)).astype(BF)
    sel = lax.dot_general(sel_true, perm, NT, preferred_element_type=F32).astype(BF)
    count = sel_slot.shape[0]
    sel_slot[...] = sel[:count]
    sel_own[...] = sel[count:]
    hot = pos[0:1, :] == iota((cores * pe, 1), 0).astype(F32)
    expand[...] = hot.astype(BF)
    mine = jnp.sum(jnp.where(hot, own_share, 0.0), axis=1, keepdims=True)
    share[...] = jnp.broadcast_to(mine, share.shape)


def project_kernel(n, *refs):
    ys = refs[:n]
    sel_slot, sel_own, w = refs[n : n + 3]
    *outs, y_all, y_sel = refs[-6:]
    size = ys[0].shape[0]
    for q in range(n):
        y_all[q * size : (q + 1) * size, :] = ys[q][...]
    at = 0
    for sel in (sel_slot, sel_own):
        got = jnp.dot(sel[...], y_all[...], preferred_element_type=F32).astype(BF)
        y_sel[at : at + got.shape[0], :] = got
        at += got.shape[0]
    wb = min(512, w.shape[1])

    @pl.loop(0, w.shape[1] // wb)
    def _(g):
        at = pl.ds(pl.multiple_of(g * wb, wb), wb)
        out = jnp.dot(y_sel[...], w[:, at], preferred_element_type=F32).astype(BF)
        row = 0
        for part in outs:
            part[:, at] = out[row : row + part.shape[0]]
            row += part.shape[0]


def project(n, ys, sel_slot, sel_own, w, dep):
    vm = pl.BlockSpec(memory_space=pltpu.VMEM)
    slot, total = sel_slot.shape
    own = sel_own.shape[0]
    ch, wc = w.shape
    return pl.pallas_call(
        functools.partial(project_kernel, n),
        in_specs=[vm] * (n + 3) + [pl.BlockSpec(memory_space=pl.ANY)],
        out_specs=[vm] * 4,
        out_shape=[jax.ShapeDtypeStruct((slot // 2, wc), BF)] * 2
        + [jax.ShapeDtypeStruct((own // 2, wc), BF)] * 2,
        scratch_shapes=[pltpu.VMEM((total, ch), BF), pltpu.VMEM((slot + own, ch), BF)],
        compiler_params=params(10),
        cost_estimate=cost(1e5, 1 << 12),
        name="project",
    )(*ys, sel_slot, sel_own, w, dep)


def load_kernel(chunks, w, *refs):
    out, token, sem = refs[-3:]
    token[...] = jnp.zeros_like(token)
    size = w.shape[0] // chunks
    copies = [
        pltpu.make_async_copy(
            w.at[pl.ds(q * size, size)], out.at[pl.ds(q * size, size)], sem.at[q]
        )
        for q in range(chunks)
    ]
    for copy in copies:
        copy.start()
    for copy in copies:
        copy.wait()


def fetch_kernel(count, *refs):
    srcs, outs, sem = refs[:count], refs[-count - 1 : -1], refs[-1]
    copies = [pltpu.make_async_copy(srcs[q], outs[q], sem.at[q]) for q in range(count)]
    for copy in copies:
        copy.start()
    for copy in copies:
        copy.wait()


def gate_kernel(m, me, *refs):
    pieces = 2 * m
    xs = refs[:pieces]
    share, gw, uw, act, x_scr, ubuf, usem = refs[pieces:]
    pe = xs[0].shape[0]
    ub, deep = ubuf.shape[2], ubuf.shape[0]
    nu = gw.shape[1] // ub

    def up_copy(j):
        return pltpu.make_async_copy(
            uw.at[:, pl.ds(pl.multiple_of(j * ub, ub), ub)],
            ubuf.at[lax.rem(j, deep)],
            usem.at[lax.rem(j, deep)],
        )

    for j in range(min(deep, nu)):
        up_copy(j).start()
    first = me[2] == 0
    for kz in range(m):
        own, other = xs[2 * kz][...].astype(F32), xs[2 * kz + 1][...].astype(F32)
        pair = jnp.concatenate(
            [jnp.where(first, own, other), jnp.where(first, other, own)], axis=0
        ).astype(BF)
        at = pl.multiple_of((me[1] ^ kz) * (2 * pe), 2 * pe)
        x_scr[pl.ds(at, 2 * pe), :] = pair

    @pl.loop(0, nu)
    def _(j):
        at = pl.ds(pl.multiple_of(j * ub, ub), ub)
        gated = jnp.dot(x_scr[...], gw[:, at], preferred_element_type=F32)
        up_copy(j).wait()
        upped = jnp.dot(x_scr[...], ubuf[lax.rem(j, deep)], preferred_element_type=F32)

        @pl.when(j + deep < nu)
        def _():
            up_copy(j + deep).start()

        act[:, at] = (gated * jax.nn.sigmoid(gated) * upped * share[:, 0:1]).astype(BF)


def down_kernel(m, deps, me, act, dw, *refs):
    send, keep, dbuf, dsem = refs[deps:]
    pc, deep = dbuf.shape[2], dbuf.shape[0]
    nh = send.shape[1] // pc
    cut = nh // m
    nd = 2 * nh

    def down_copy(i):
        h, j = jnp.where(i < nh, 1, 0), lax.rem(i, nh)
        block = ((me[2] ^ h) * m + (me[1] ^ lax.div(j, cut))) * cut + lax.rem(j, cut)
        return pltpu.make_async_copy(
            dw.at[:, pl.ds(pl.multiple_of(block * pc, pc), pc)],
            dbuf.at[lax.rem(i, deep)],
            dsem.at[lax.rem(i, deep)],
        )

    for i in range(min(deep, nd)):
        down_copy(i).start()

    @pl.loop(0, nd)
    def _(i):
        down_copy(i).wait()
        out = jnp.dot(act[...], dbuf[lax.rem(i, deep)], preferred_element_type=F32).astype(BF)
        at = pl.ds(pl.multiple_of(lax.rem(i, nh) * pc, pc), pc)

        @pl.when(i < nh)
        def _():
            send[:, at] = out

        @pl.when(i >= nh)
        def _():
            keep[:, at] = out

        @pl.when(i + deep < nd)
        def _():
            down_copy(i + deep).start()


def pair_rows_kernel(count, keep, got, *refs):
    outs = refs[-count:]
    size = outs[0].shape[0]
    for k in range(count):
        at = slice(k * size, (k + 1) * size)
        both = keep[at].astype(F32) + got[at].astype(F32)
        outs[k][...] = both.astype(outs[k].dtype)


def pair_cols_kernel(count, keep, got, *refs):
    outs = refs[-count:]
    size = outs[0].shape[1]
    for k in range(count):
        at = slice(k * size, (k + 1) * size)
        both = keep[:, at].astype(F32) + got[:, at].astype(F32)
        outs[k][...] = both.astype(outs[k].dtype)


def sum_rows_kernel(count, parts, *refs):
    outs = refs[-parts:]
    size = outs[0].shape[0]
    total = refs[0][...]
    for k in range(1, count):
        total = total + refs[k][...].astype(F32)
    for k in range(parts):
        outs[k][...] = total[k * size : (k + 1) * size].astype(BF)


def norm_kernel(n, me, gain, *refs):
    hid, out = refs[:n], refs[n]
    wc = hid[0].shape[1]
    wide = [h[...].astype(F32) for h in hid]
    square = sum(jnp.sum(h * h, axis=1, keepdims=True) for h in wide)
    scale = lax.rsqrt(square / (n * wc) + 1e-05)
    for k in range(n):
        at = pl.ds(pl.multiple_of((me[0] ^ k) * wc, wc), wc)
        out[:, at] = (wide[k] * scale * gain[:, at]).astype(BF)


def spread_kernel(n, m, me, expand, *refs):
    outs, scr = refs[-n - 1 : -1], refs[-1]
    out = refs[0][...]
    for k in range(1, m):
        out = out + refs[k][...].astype(F32)
    scr[...] = lax.dot_general(expand[...], out.astype(BF), TN, preferred_element_type=F32)
    size = outs[0].shape[0]
    for k in range(n):
        got = scr[pl.ds(pl.multiple_of((me[0] ^ k) * size, size), size), :]
        outs[k][...] = got.astype(outs[k].dtype)


def deal_kernel(n, m, me, *refs):
    keep, send, scr = refs[n:]
    total = refs[0][...]
    for k in range(1, n):
        total = total + refs[k][...].astype(F32)
    scr[...] = total
    rm = keep.shape[0] // m
    for q in range(2 * m):
        block = (me[1] ^ (q // 2)) * 2 + (me[2] ^ (q % 2))
        out = send if q % 2 else keep
        if rm % 8 == 0:
            got = scr[pl.ds(pl.multiple_of(block * rm, rm), rm), :]
        else:
            got = scr[:rm]
            for b in range(1, 2 * m):
                got = jnp.where(block == b, scr[b * rm : (b + 1) * rm], got)
        out[(q // 2) * rm : (q // 2 + 1) * rm, :] = got.astype(BF)


def pair_kernel(m, keep, got, *outs):
    rm = outs[0].shape[0]
    pc = keep.shape[1]
    for k in range(m):
        outs[k][:, :pc] = keep[k * rm : (k + 1) * rm]
        outs[k][:, pc:] = got[k * rm : (k + 1) * rm]


def hold_kernel(*refs):
    pass


def small(kern, name, outs, args, deps=(), scr=()):
    vm = pl.BlockSpec(memory_space=pltpu.VMEM)
    sm = pl.BlockSpec(memory_space=pltpu.SMEM)
    count = len(args)

    def run(*refs):
        kern(*refs[:count], *refs[count + len(deps) :])

    specs = [sm if a.dtype == jnp.int32 and a.ndim == 1 else vm for a in args]
    return pl.pallas_call(
        run,
        in_specs=specs + [pl.BlockSpec(memory_space=pl.ANY)] * len(deps),
        out_specs=[vm] * len(outs),
        out_shape=[jax.ShapeDtypeStruct(*o) for o in outs],
        scratch_shapes=list(scr),
        compiler_params=params(8),
        cost_estimate=cost(1e5, 1 << 12),
        name=name,
    )(*args, *deps)


def place_kernel(n, states, me, rr, *refs):
    srcs, (out, token, buf, sem) = refs[:n], refs[-4:]
    token[...] = jnp.zeros_like(token)
    i, last = pl.program_id(0), pl.num_programs(0) - 1
    slot = lax.rem(i, 2)

    def copies(step, where):
        return [
            pltpu.make_async_copy(buf.at[where, k], out.at[rr[0, me[0] ^ k, step]], sem.at[where, k])
            for k in range(n)
        ]

    @pl.when(i >= 2)
    def _():
        for copy in copies(i - 2, slot):
            copy.wait()

    for k in range(n):
        buf[slot, k] = srcs[k][...].astype(F32)
    for copy in copies(i, slot):
        copy.start()

    @pl.when(i == last)
    def _():
        for copy in copies(i - 1, 1 - slot):
            copy.wait()
        for copy in copies(i, slot):
            copy.wait()


def place(n, per, rows, states, me, rr, srcs, dep):
    ch = srcs[0].shape[1]
    return pl.pallas_call(
        functools.partial(place_kernel, n, states),
        grid_spec=pltpu.PrefetchScalarGridSpec(
            num_scalar_prefetch=2,
            grid=(per,),
            in_specs=[pl.BlockSpec((states, ch), lambda i, *_: (i, 0))] * n
            + [pl.BlockSpec(memory_space=pl.ANY)],
            out_specs=[
                pl.BlockSpec(memory_space=pl.ANY),
                pl.BlockSpec((8, 128), lambda i, *_: (0, 0)),
            ],
            scratch_shapes=[
                pltpu.VMEM((2, n, states, ch), F32),
                pltpu.SemaphoreType.DMA((2, n)),
            ],
        ),
        out_shape=[
            jax.ShapeDtypeStruct((rows, states, ch), F32),
            jax.ShapeDtypeStruct((8, 128), F32),
        ],
        compiler_params=params(8),
        cost_estimate=cost(1e5, 1 << 12),
        name="place",
    )(me, rr, *srcs, dep)


def tail_kernel(n, per, taps, me, rr, x, *refs):
    tails, (out, token) = refs[:n], refs[-2:]
    token[...] = jnp.zeros_like(token)
    steps = x.shape[0]
    keep = taps - steps
    for t in range(steps):
        out[keep + t] = x[t].astype(F32)
    for k in range(n):
        block = tails[k][...].astype(F32)
        for j in range(keep):
            for i in range(per):
                q = j * per + i
                out[j, pl.ds(rr[0, me[0] ^ k, i], 1), :] = block[q : q + 1, :]


def final_kernel(n, m, me, *refs):
    hid = refs[:n]
    parts = refs[n : n + m]
    out, acc = refs[-2:]
    wc = hid[0].shape[1]
    for k in range(n):
        acc[:, pl.ds(pl.multiple_of((me[0] ^ k) * wc, wc), wc)] = hid[k][...].astype(F32)
    pc = parts[0].shape[1] // 2
    for q in range(2 * m):
        zs, h = me[1] ^ (q // 2), q % 2
        where = pl.ds(pl.multiple_of(((me[2] ^ h) * m + zs) * pc, pc), pc)
        got = parts[q // 2][:, h * pc : (h + 1) * pc].astype(F32)
        acc[:, where] = acc[:, where] + got
    out[...] = acc[...].astype(BF)


def body(
    conv_cache,
    state_cache,
    send_slot,
    recv_row,
    prefix_length,
    x_input,
    z_input,
    dt_input,
    b_input,
    c_input,
    conv_weight,
    conv_bias,
    dt_bias,
    decay_rate,
    skip_gain,
    out_weight,
    norm_gain,
    route_ids,
    route_weight,
    expert_slots,
    gate_weight,
    up_weight,
    down_weight,
):
    n = lax.axis_size("dp")
    m = lax.axis_size("z")
    d, zz, cc = lax.axis_index("dp"), lax.axis_index("z"), lax.axis_index("core")
    me = jnp.stack([d, zz, cc]).astype(jnp.int32)
    steps, rows, ch = x_input.shape
    per = rows // n
    taps = conv_cache.shape[1]
    states = state_cache.shape[1]
    total = steps * n * rows
    cap = total // 4
    pe = cap // (2 * m)
    rm = total // (n * 2 * m)
    width = gate_weight.shape[1]
    wc = out_weight.shape[1]
    dm = n * wc
    rr, ss = recv_row, send_slot
    vm = pl.BlockSpec(memory_space=pltpu.VMEM)
    sm = pl.BlockSpec(memory_space=pltpu.SMEM)

    in_hbm = functools.partial(pltpu.with_memory_space_constraint, memory_space=pltpu.HBM)

    def whole(a):
        return pl.BlockSpec(a.shape, lambda g: (0,) * a.ndim)

    src = (
        x_input,
        z_input,
        dt_input,
        jnp.transpose(b_input, (0, 2, 1)),
        jnp.transpose(c_input, (0, 2, 1)),
        prefix_length.reshape(1, rows),
    )
    src = [in_hbm(a) for a in src]
    packed = jax.ShapeDtypeStruct((per, 3 * steps * ch + META), BF)
    payload = pl.pallas_call(
        functools.partial(pack_kernel, n, per),
        grid=(1,),
        in_specs=[sm, sm] + [whole(a) for a in src],
        out_specs=[whole(packed)] * n,
        out_shape=[packed] * n,
        scratch_shapes=[pltpu.VMEM((128, rows), F32)],
        compiler_params=params(12),
        cost_estimate=cost(1e6, 2 << 20),
        name="pack",
    )(me, recv_row, *src)
    payload = [payload[0]] + [trade(payload[k], "dp", n, k) for k in range(1, n)]
    par = jnp.concatenate(
        [conv_weight, conv_bias[None], dt_bias[None], skip_gain[None], jnp.zeros((1, ch), F32)], 0
    )
    conv = jnp.transpose(conv_cache, (1, 0, 2))
    fixed = (par, decay_rate, conv, state_cache)
    hbm = pl.BlockSpec(memory_space=pltpu.HBM)
    fixed = pl.pallas_call(
        functools.partial(fetch_kernel, len(fixed)),
        in_specs=[hbm] * len(fixed) + [pl.BlockSpec(memory_space=pl.ANY)],
        out_specs=[vm] * len(fixed),
        out_shape=[pltpu.VMEM(a.shape, a.dtype) for a in fixed],
        scratch_shapes=[pltpu.SemaphoreType.DMA((len(fixed),))],
        compiler_params=params(1),
        cost_estimate=cost(1e5, 1 << 12),
        name="fetch",
    )(*[in_hbm(a) for a in fixed], payload[0])
    y_own, *kept = ssm(per, steps, me, ss, payload, *fixed)
    ys = [y_own] + [trade(y_own, "dp", n, k) for k in range(1, n)]

    n_slot, n_own = 2 * m * n * pe, 2 * m * n * rm
    ids_t = route_ids.reshape(total, -1).T
    wts_t = route_weight.reshape(total, -1).T
    meta_at = 3 * steps * ch // 128
    sel_slot, sel_own, share, expand = pl.pallas_call(
        functools.partial(select_kernel, n, m, per, steps, rows, rm, pe, width),
        grid=(1,),
        in_specs=[sm, sm]
        + [pl.BlockSpec(ids_t.shape, lambda g: (0, 0))] * 2
        + [pl.BlockSpec((per, 128), lambda g: (0, meta_at))] * n,
        out_specs=[
            pl.BlockSpec((n_slot, total), lambda g: (0, 0)),
            pl.BlockSpec((n_own, total), lambda g: (0, 0)),
            pl.BlockSpec((cap, 128), lambda g: (0, 0)),
            pl.BlockSpec((cap, total), lambda g: (0, 0)),
        ],
        out_shape=[
            jax.ShapeDtypeStruct((n_slot, total), BF),
            jax.ShapeDtypeStruct((n_own, total), BF),
            jax.ShapeDtypeStruct((cap, 128), F32),
            jax.ShapeDtypeStruct((cap, total), BF),
        ],
        compiler_params=params(10),
        cost_estimate=cost(1e7, 1 << 20),
        name="select",
    )(me, expert_slots, ids_t, wts_t, *payload)

    width = gate_weight.shape[1]
    chunks = 8
    gate_here, loaded = pl.pallas_call(
        functools.partial(load_kernel, chunks),
        in_specs=[pl.BlockSpec(memory_space=pltpu.HBM), pl.BlockSpec(memory_space=pl.ANY)],
        out_specs=[vm, vm],
        out_shape=[pltpu.VMEM(gate_weight.shape, BF), jax.ShapeDtypeStruct((8, 128), F32)],
        scratch_shapes=[pltpu.SemaphoreType.DMA((chunks,))],
        compiler_params=params(1),
        cost_estimate=cost(1e5, 1 << 12),
        name="load",
    )(in_hbm(gate_weight), y_own)
    anyspace = pl.BlockSpec(memory_space=pl.ANY)

    def add_core(keep, send, each, name, dep=()):
        got = trade(send, "core", 2, 1)
        shape = (n * each, wc)
        outs = [(shape, F32)] + [(shape, BF)] * (m - 1)
        return small(functools.partial(pair_rows_kernel, m), name, outs, (keep, got), dep)

    def send_z(parts):
        return [parts[0]] + [trade(parts[k], "z", m, k) for k in range(1, m)]

    def add_z(got, each, name, dep=()):
        outs = [((each, wc), BF)] * n
        out = small(functools.partial(sum_rows_kernel, len(got), n), name, outs, got, dep)
        return [out[0]] + [trade(out[k], "dp", n, k) for k in range(1, n)]

    keep_slot, send_slot_rows, keep_own, send_own = project(
        n, ys, sel_slot, sel_own, out_weight, loaded
    )
    parts = add_core(keep_slot, send_slot_rows, pe, "core_slot")
    slot_z = send_z(parts)
    hid = add_z(slot_z, pe, "z_slot")
    [normed] = small(
        functools.partial(norm_kernel, n),
        "norm",
        [((pe, dm), BF)],
        (me, norm_gain.reshape(1, dm), *hid),
    )
    near = [normed] + [trade(normed, "z", m, k) for k in range(1, m)]
    xs = []
    for piece in near:
        xs += [piece, trade(piece, "core", 2, 1)]
    size = m * n * rm // 2
    halves = [((size, wc), F32), ((size, wc), BF)]
    own_keep, own_send = small(
        functools.partial(pair_rows_kernel, 2),
        "core_own",
        halves,
        (keep_own, trade(send_own, "core", 2, 1)),
        (near[1],),
    )
    held = pl.pallas_call(
        hold_kernel,
        in_specs=[anyspace] * n,
        out_specs=[anyspace] * (n - 1),
        out_shape=[jax.ShapeDtypeStruct(k.shape, k.dtype) for k in kept[1:]],
        input_output_aliases={k: k for k in range(n - 1)},
        compiler_params=params(1),
        name="hold",
    )(*kept[1:], near[1])
    back = [kept[0]] + [trade(held[k - 1], "dp", n, k) for k in range(1, n)]

    half = dm // 2
    pc = half // m
    ub = 256 if width % 256 == 0 else 128
    act = pl.pallas_call(
        functools.partial(gate_kernel, m),
        in_specs=[sm] + [vm] * (2 * m + 2) + [pl.BlockSpec(memory_space=pltpu.HBM)],
        out_specs=vm,
        out_shape=jax.ShapeDtypeStruct((cap, width), BF),
        scratch_shapes=[
            pltpu.VMEM((cap, dm), BF),
            pltpu.VMEM((2, dm, ub), BF),
            pltpu.SemaphoreType.DMA((2,)),
        ],
        compiler_params=params(14),
        cost_estimate=cost(4 * cap * dm * width, 4 * dm * width),
        name="gate",
    )(me, *xs, share, gate_here, in_hbm(up_weight))
    k = m // 2
    while k > 1:
        size //= 2
        own_keep, own_send = small(
            functools.partial(pair_rows_kernel, 2),
            f"half{k}",
            [((size, wc), F32), ((size, wc), BF)],
            (own_keep, trade(own_send, "z", m, k)),
        )
        k //= 2
    own_z = [own_keep, trade(own_send, "z", m, 1)]
    deps = [own_send] + back[1:]
    send, keep = pl.pallas_call(
        functools.partial(down_kernel, m, len(deps)),
        in_specs=[sm, vm, pl.BlockSpec(memory_space=pltpu.HBM)] + [anyspace] * len(deps),
        out_specs=[vm] * 2,
        out_shape=[jax.ShapeDtypeStruct((cap, half), BF)] * 2,
        scratch_shapes=[pltpu.VMEM((6, width, pc // 2), BF), pltpu.SemaphoreType.DMA((6,))],
        compiler_params=params(14),
        cost_estimate=cost(2 * cap * dm * width, 2 * dm * width),
        name="down",
    )(me, act, in_hbm(down_weight), *deps)

    got = trade(send, "core", 2, 1)
    outs = [((cap, pc), F32)] + [((cap, pc), BF)] * (m - 1)
    cols = small(functools.partial(pair_cols_kernel, m), "core_out", outs, (keep, got))
    moved = [cols[0]] + [trade(cols[k], "z", m, k) for k in range(1, m)]

    own = add_z(own_z, rm, "z_own", (cols[1],))
    share_rows = total // n
    outs = [((share_rows, pc), F32)] + [((share_rows, pc), BF)] * (n - 1)
    rows_out = small(
        functools.partial(spread_kernel, n, m),
        "spread",
        outs,
        (me, expand, *moved),
        tuple(own[1:]),
        [pltpu.VMEM((total, pc), F32)],
    )
    new_state, placed = place(n, per, rows, states, me, rr, back, rows_out[1])
    low = kept[0].shape[0] - per * states
    tail_at = per * states // low
    new_tail, placed = pl.pallas_call(
        functools.partial(tail_kernel, n, per, taps),
        grid=(1,),
        in_specs=[sm, sm, pl.BlockSpec(x_input.shape, lambda g: (0, 0, 0))]
        + [pl.BlockSpec((low, ch), lambda g: (tail_at, 0))] * n
        + [anyspace],
        out_specs=[
            pl.BlockSpec((taps, rows, ch), lambda g: (0, 0, 0)),
            pl.BlockSpec((8, 128), lambda g: (0, 0)),
        ],
        out_shape=[
            jax.ShapeDtypeStruct((taps, rows, ch), F32),
            jax.ShapeDtypeStruct((8, 128), F32),
        ],
        compiler_params=params(8),
        cost_estimate=cost(1e5, 1 << 12),
        name="tail",
    )(me, rr, x_input, *back, placed)

    mine = [rows_out[0]] + [trade(rows_out[k], "dp", n, k) for k in range(1, n)]
    deal_keep, deal_send = small(
        functools.partial(deal_kernel, n, m),
        "deal",
        [((m * rm, pc), BF)] * 2,
        (me, *mine),
        (placed,),
        [pltpu.VMEM((share_rows, pc), F32)],
    )
    pieces = small(
        functools.partial(pair_kernel, m),
        "pair",
        [((rm, 2 * pc), BF)] * m,
        (deal_keep, trade(deal_send, "core", 2, 1)),
    )
    pieces = send_z(pieces)
    [mixed] = small(
        functools.partial(final_kernel, n, m),
        "final",
        [((rm, dm), BF)],
        (me, *own, *pieces),
        (),
        [pltpu.VMEM((rm, dm), F32)],
    )
    return (mixed, new_state, jnp.transpose(new_tail, (1, 0, 2)))


def solution(mesh):
    n = mesh.shape["dp"]
    m = mesh.shape["expert"] // 2
    split = Mesh(mesh.devices.reshape(n, m, 2), ("dp", "z", "core"))
    e = ("z", "core")
    de = ("dp", "z", "core")
    in_specs = (
        P("dp", None, e),
        P("dp", None, e),
        P(),
        P("dp", None, None),
        P("dp"),
        P(None, "dp", e),
        P(None, "dp", e),
        P(None, "dp", e),
        P(None, "dp", None),
        P(None, "dp", None),
        P(None, e),
        P(e),
        P(e),
        P(None, e),
        P(e),
        P(e, "dp"),
        P(),
        P(),
        P(),
        P(),
        P(None, de),
        P(None, de),
        P(de, None),
    )
    out_specs = (P(de, None), P("dp", None, e), P("dp", None, e))
    return jax.shard_map(body, mesh=split, in_specs=in_specs, out_specs=out_specs, check_vma=False)
```

```python
import functools

import jax
import jax.numpy as jnp
from jax import lax
from jax.experimental import pallas as pl
from jax.experimental.pallas import tpu as pltpu
from jax.sharding import Mesh
from jax.sharding import PartitionSpec as P

FFW = 12288
BF = jnp.bfloat16
F32 = jnp.float32
META = 256
TABLE = 96
PREFIX = 64
NT = (((1,), (1,)), ((), ()))
TN = (((0,), (0,)), ((), ()))


def cost(flops, moved):
    return pl.CostEstimate(flops=int(flops), bytes_accessed=int(moved), transcendentals=0)


def params(limit):
    return pltpu.CompilerParams(vmem_limit_bytes=limit << 20)


def iota(shape, dim):
    return lax.broadcasted_iota(jnp.int32, shape, dim)


def trade(piece, axis, size, k):
    return lax.ppermute(piece, axis, [(i, i ^ k) for i in range(size)])


def pack_kernel(n, per, me, rr, x, z, dt, b, c, prefix, *rest):
    outs, m_scr = rest[:n], rest[n]
    steps, rows, ch = x.shape
    states = b.shape[1]
    m_scr[...] = jnp.zeros_like(m_scr)
    for t in range(steps):
        m_scr[2 * t * states : (2 * t + 1) * states, :] = b[t]
        m_scr[(2 * t + 1) * states : (2 * t + 2) * states, :] = c[t]
    m_scr[PREFIX : PREFIX + 1, :] = prefix[...].astype(F32)
    rowcol = jnp.zeros((n * per, 1), jnp.int32)
    table = jnp.zeros((1, 128), F32)
    sub = iota((n * per, 1), 0)
    lane = iota((1, 128), 1)
    for k in range(n):
        for i in range(per):
            rowcol = jnp.where(sub == k * per + i, rr[0, me[0] ^ k, i], rowcol)
            q = k * per + i
            table = jnp.where(lane == TABLE + q, rr[0, k, i].astype(F32), table)
    hot = rowcol == iota((n * per, rows), 1)
    hot_b = hot.astype(BF)
    for a, src in enumerate((x, z, dt)):
        for t in range(steps):
            got = jnp.dot(hot_b, src[t], preferred_element_type=F32).astype(BF)
            at = (a * steps + t) * ch
            for k in range(n):
                outs[k][:, at : at + ch] = got[k * per : (k + 1) * per]
    meta = lax.dot_general(
        hot.astype(F32), m_scr[...], NT, precision=lax.Precision.HIGHEST, preferred_element_type=F32
    )
    meta = meta + table
    hi = meta.astype(BF)
    lo = (meta - hi.astype(F32)).astype(BF)
    at = 3 * steps * ch
    for k in range(n):
        outs[k][:, at : at + 128] = hi[k * per : (k + 1) * per]
        outs[k][:, at + 128 : at + 256] = lo[k * per : (k + 1) * per]


def ssm_kernel(first, groups, per, steps, me, ss, *refs):
    if first:
        y_first, refs = refs[0], refs[1:]
    loads = refs[:groups]
    par, decay, conv, state, y_out = refs[groups : groups + 5]
    st_outs = refs[groups + 5 : 2 * groups + 5]
    y_scr, tail_scr, bc_scr, du_scr = refs[2 * groups + 5 :]
    taps, _, ch = conv.shape
    states = decay.shape[0]
    cb = y_scr.shape[2]
    lb = min(256, cb)
    low = st_outs[0].shape[0] - per * states
    done = 0
    if first:
        done = y_first.shape[0]
        y_out[:done, :] = y_first[...]
    at = 3 * steps * ch
    masks = []
    for q in range(groups):
        val = loads[q][:, at : at + 128].astype(F32) + loads[q][:, at + 128 : at + 256].astype(F32)
        full = jnp.concatenate([val, jnp.zeros((128 - per, 128), F32)], axis=0)
        bc_scr[q] = jnp.transpose(full)
        prefix = val[:, PREFIX : PREFIX + 1]
        masks.append([(prefix >= float(taps - j)).astype(F32) for j in range(taps)])

    @pl.loop(0, ch // cb)
    def _(g):
        base = pl.multiple_of(g * cb, cb)
        wide = pl.ds(base, cb)
        for q in range(groups):
            slots = [ss[me[0], me[0] ^ (q + first), i] for i in range(per)]

            def load(a):
                return loads[q][:, pl.ds(pl.multiple_of(a * ch + base, cb), cb)].astype(F32)

            for j in range(taps):
                for i in range(per):
                    tail_scr[j, i : i + 1, :] = conv[j, pl.ds(slots[i], 1), wide]
            window = [tail_scr[j] * masks[q][j] for j in range(taps)]
            skips, gates = [], []
            for t in range(steps):
                window.append(load(t))
                acc = window[t] * par[0:1, wide]
                for j in range(1, taps + 1):
                    acc = acc + window[t + j] * par[j : j + 1, wide]
                acc = acc + par[taps + 1 : taps + 2, wide]
                xc = acc * jax.nn.sigmoid(acc)
                raw = load(2 * steps + t) + par[taps + 2 : taps + 3, wide]
                delta = jnp.maximum(raw, 0.0) + jnp.log1p(jnp.exp(-jnp.abs(raw)))
                zt = load(steps + t)
                du_scr[2 * t] = delta * -1.4426950408889634
                du_scr[2 * t + 1] = delta * xc
                skips.append(par[taps + 3 : taps + 4, wide] * xc)
                gates.append(zt * jax.nn.sigmoid(zt))
            kept = window[steps:taps]
            kept.append(jnp.zeros((low - per * len(kept), cb), F32))
            kept = jnp.concatenate(kept, axis=0)
            st_outs[q][per * states :, wide] = kept.astype(st_outs[q].dtype)
            for i in range(per):
                cols = []
                for k in range(2 * steps):
                    col = bc_scr[q, k * states : (k + 1) * states, i : i + 1]
                    cols.append(jnp.broadcast_to(col, (states, lb)))
                for l in range(cb // lb):
                    here = slice(l * lb, (l + 1) * lb)
                    there = pl.ds(pl.multiple_of(base + l * lb, lb), lb)
                    st = state[slots[i], :, there]
                    for t in range(steps):
                        dl = du_scr[2 * t, i : i + 1, here]
                        ul = du_scr[2 * t + 1, i : i + 1, here]
                        st = jnp.exp2(dl * decay[:, there]) * st + ul * cols[2 * t]
                        y_scr[t, i : i + 1, here] = jnp.sum(
                            cols[2 * t + 1] * st, axis=0, keepdims=True
                        )
                    st_outs[q][i * states : (i + 1) * states, there] = st.astype(st_outs[q].dtype)
            for t in range(steps):
                row = done + (q * steps + t) * per
                y_out[row : row + per, wide] = ((y_scr[t] + skips[t]) * gates[t]).astype(BF)


def ssm(first, per, steps, me, ss, payloads, par, decay, conv, state):
    groups = len(payloads)
    states, ch = decay.shape
    cb = ch // 4
    taps = conv.shape[0]
    low = -(-(taps - steps) * per // 16) * 16
    vm = pl.BlockSpec(memory_space=pltpu.VMEM)
    sm = pl.BlockSpec(memory_space=pltpu.SMEM)
    args = list(payloads) + [par, decay, conv, state]
    groups -= first
    return pl.pallas_call(
        functools.partial(ssm_kernel, first, groups, per, steps),
        in_specs=[sm, sm] + [vm] * len(args),
        out_specs=[vm] * (1 + groups),
        out_shape=[jax.ShapeDtypeStruct(((first + groups) * steps * per, ch), BF)]
        + [
            jax.ShapeDtypeStruct((per * states + low, ch), BF if first else F32)
            for q in range(groups)
        ],
        scratch_shapes=[
            pltpu.VMEM((steps, per, cb), F32),
            pltpu.VMEM((taps, per, cb), F32),
            pltpu.VMEM((groups, 128, 128), F32),
            pltpu.VMEM((2 * steps, per, cb), F32),
        ],
        compiler_params=params(4),
        cost_estimate=cost(3e6 * groups, groups * 3 << 20),
        name=f"ssm{first}",
    )(me, ss, *args)


def select_kernel(n, m, per, steps, rows, rm, pe, width, me, es, ids, wts, *refs):
    tables = refs[:n]
    sel_slot, sel_own, share, expand = refs[n:]
    cores = m * 2
    d, zz, cc = me[0], me[1], me[2]
    total = steps * n * rows
    choices = ids.shape[0]
    sub8 = iota((8, total), 0)
    match = jnp.zeros((8, total), F32)
    own_share = jnp.zeros((1, total), F32)
    hits = []
    for kd in range(n):
        eid = es[((d ^ kd) * (cores * width)) // FFW]
        hit = jnp.zeros((1, total), F32)
        for q in range(choices):
            same = ids[q : q + 1, :] == eid
            hit = jnp.where(same, 1.0, hit)
            if kd == 0:
                own_share = own_share + jnp.where(same, wts[q : q + 1, :], 0.0)
        hits.append(hit)
        match = jnp.where(sub8 == kd, hit, match)
    before = (iota((total, total), 0) < iota((total, total), 1)).astype(BF)
    pos = jnp.dot(match.astype(BF), before, preferred_element_type=F32)
    pos = jnp.where(match > 0.0, pos, -1.0)
    col = iota((pe, 1), 0)
    parts, owns = [], []
    for h in range(2):
        for kz in range(m):
            first = ((zz ^ kz) * 2 + (cc ^ h)) * pe
            want = (col + first).astype(F32)
            for kd in range(n):
                parts.append((pos[kd : kd + 1, :] == want).astype(BF))
        row = iota((m * n * rm, 1), 0)
        kz_v = row // (n * rm)
        kd_v = (row // rm) % n
        true = ((d ^ kd_v) * cores + (zz ^ kz_v) * 2 + (cc ^ h)) * rm + row % rm
        owns.append((true == iota((m * n * rm, total), 1)).astype(BF))
    sel_true = jnp.concatenate(parts + owns, axis=0)
    j = iota((total, 1), 0)
    ko = j // (n * steps * per)
    kd = (j // (steps * per)) % n
    tab = jnp.zeros((8, 128), F32)
    for q in range(n):
        tab = jnp.where(iota((8, 128), 0) == q, tables[q][0:1, :].astype(F32), tab)
    pick = (iota((total, 8), 1) == (ko ^ kd)).astype(BF)
    tj = jnp.dot(pick, tab.astype(BF), preferred_element_type=F32)
    lane = TABLE + (d ^ ko) * per + j % per
    local = jnp.sum(jnp.where(iota((total, 128), 1) == lane, tj, 0.0), axis=1, keepdims=True)
    true = ((j // per) % steps) * (n * rows) + (d ^ ko ^ kd) * rows + local.astype(jnp.int32)
    perm = (true == iota((total, total), 1)).astype(BF)
    sel = lax.dot_general(sel_true, perm, NT, preferred_element_type=F32).astype(BF)
    count = sel_slot.shape[0]
    sel_slot[...] = sel[:count]
    sel_own[...] = sel[count:]
    hot = pos[0:1, :] == iota((cores * pe, 1), 0).astype(F32)
    expand[...] = hot.astype(BF)
    mine = jnp.sum(jnp.where(hot, own_share, 0.0), axis=1, keepdims=True)
    share[...] = jnp.broadcast_to(mine, share.shape)


def project_kernel(n, *refs):
    ys = refs[:n]
    sel_slot, sel_own, w = refs[n : n + 3]
    *outs, y_all, y_sel = refs[-6:]
    size = ys[0].shape[0]
    for q in range(n):
        y_all[q * size : (q + 1) * size, :] = ys[q][...]
    at = 0
    for sel in (sel_slot, sel_own):
        got = jnp.dot(sel[...], y_all[...], preferred_element_type=F32).astype(BF)
        y_sel[at : at + got.shape[0], :] = got
        at += got.shape[0]
    wb = min(512, w.shape[1])

    @pl.loop(0, w.shape[1] // wb)
    def _(g):
        at = pl.ds(pl.multiple_of(g * wb, wb), wb)
        out = jnp.dot(y_sel[...], w[:, at], preferred_element_type=F32).astype(BF)
        row = 0
        for part in outs:
            part[:, at] = out[row : row + part.shape[0]]
            row += part.shape[0]


def project(n, ys, sel_slot, sel_own, w, dep):
    vm = pl.BlockSpec(memory_space=pltpu.VMEM)
    slot, total = sel_slot.shape
    own = sel_own.shape[0]
    ch, wc = w.shape
    return pl.pallas_call(
        functools.partial(project_kernel, n),
        in_specs=[vm] * (n + 3) + [pl.BlockSpec(memory_space=pl.ANY)],
        out_specs=[vm] * 4,
        out_shape=[jax.ShapeDtypeStruct((slot // 2, wc), BF)] * 2
        + [jax.ShapeDtypeStruct((own // 2, wc), BF)] * 2,
        scratch_shapes=[pltpu.VMEM((total, ch), BF), pltpu.VMEM((slot + own, ch), BF)],
        compiler_params=params(10),
        cost_estimate=cost(1e5, 1 << 12),
        name="project",
    )(*ys, sel_slot, sel_own, w, dep)


def load_kernel(chunks, w, *refs):
    out, token, sem = refs[-3:]
    token[...] = jnp.zeros_like(token)
    size = w.shape[0] // chunks
    copies = [
        pltpu.make_async_copy(
            w.at[pl.ds(q * size, size)], out.at[pl.ds(q * size, size)], sem.at[q]
        )
        for q in range(chunks)
    ]
    for copy in copies:
        copy.start()
    for copy in copies:
        copy.wait()


def fetch_kernel(count, *refs):
    srcs, outs, sem = refs[:count], refs[-count - 1 : -1], refs[-1]
    copies = [pltpu.make_async_copy(srcs[q], outs[q], sem.at[q]) for q in range(count)]
    for copy in copies:
        copy.start()
    for copy in copies:
        copy.wait()


def gate_kernel(m, me, *refs):
    pieces = 2 * m
    xs = refs[:pieces]
    share, gw, uw, act, x_scr, ubuf, usem = refs[pieces:]
    pe = xs[0].shape[0]
    ub, deep = ubuf.shape[2], ubuf.shape[0]
    nu = gw.shape[1] // ub

    def up_copy(j):
        return pltpu.make_async_copy(
            uw.at[:, pl.ds(pl.multiple_of(j * ub, ub), ub)],
            ubuf.at[lax.rem(j, deep)],
            usem.at[lax.rem(j, deep)],
        )

    for j in range(min(deep, nu)):
        up_copy(j).start()
    first = me[2] == 0
    for kz in range(m):
        own, other = xs[2 * kz][...].astype(F32), xs[2 * kz + 1][...].astype(F32)
        pair = jnp.concatenate(
            [jnp.where(first, own, other), jnp.where(first, other, own)], axis=0
        ).astype(BF)
        at = pl.multiple_of((me[1] ^ kz) * (2 * pe), 2 * pe)
        x_scr[pl.ds(at, 2 * pe), :] = pair

    @pl.loop(0, nu)
    def _(j):
        at = pl.ds(pl.multiple_of(j * ub, ub), ub)
        gated = jnp.dot(x_scr[...], gw[:, at], preferred_element_type=F32)
        up_copy(j).wait()
        upped = jnp.dot(x_scr[...], ubuf[lax.rem(j, deep)], preferred_element_type=F32)

        @pl.when(j + deep < nu)
        def _():
            up_copy(j + deep).start()

        act[:, at] = (gated * jax.nn.sigmoid(gated) * upped * share[:, 0:1]).astype(BF)


def down_kernel(m, deps, me, act, dw, *refs):
    send, keep, dbuf, dsem = refs[deps:]
    pc, deep = dbuf.shape[2], dbuf.shape[0]
    nh = send.shape[1] // pc
    cut = nh // m
    nd = 2 * nh

    def down_copy(i):
        h, j = jnp.where(i < nh, 1, 0), lax.rem(i, nh)
        block = ((me[2] ^ h) * m + (me[1] ^ lax.div(j, cut))) * cut + lax.rem(j, cut)
        return pltpu.make_async_copy(
            dw.at[:, pl.ds(pl.multiple_of(block * pc, pc), pc)],
            dbuf.at[lax.rem(i, deep)],
            dsem.at[lax.rem(i, deep)],
        )

    for i in range(min(deep, nd)):
        down_copy(i).start()

    @pl.loop(0, nd)
    def _(i):
        down_copy(i).wait()
        out = jnp.dot(act[...], dbuf[lax.rem(i, deep)], preferred_element_type=F32).astype(BF)
        at = pl.ds(pl.multiple_of(lax.rem(i, nh) * pc, pc), pc)

        @pl.when(i < nh)
        def _():
            send[:, at] = out

        @pl.when(i >= nh)
        def _():
            keep[:, at] = out

        @pl.when(i + deep < nd)
        def _():
            down_copy(i + deep).start()


def pair_rows_kernel(count, keep, got, *refs):
    outs = refs[-count:]
    size = outs[0].shape[0]
    for k in range(count):
        at = slice(k * size, (k + 1) * size)
        both = keep[at].astype(F32) + got[at].astype(F32)
        outs[k][...] = both.astype(outs[k].dtype)


def pair_cols_kernel(count, keep, got, *refs):
    outs = refs[-count:]
    size = outs[0].shape[1]
    for k in range(count):
        at = slice(k * size, (k + 1) * size)
        both = keep[:, at].astype(F32) + got[:, at].astype(F32)
        outs[k][...] = both.astype(outs[k].dtype)


def sum_rows_kernel(count, parts, *refs):
    outs = refs[-parts:]
    size = outs[0].shape[0]
    total = refs[0][...]
    for k in range(1, count):
        total = total + refs[k][...].astype(F32)
    for k in range(parts):
        outs[k][...] = total[k * size : (k + 1) * size].astype(BF)


def norm_kernel(n, me, gain, *refs):
    hid, out = refs[:n], refs[n]
    wc = hid[0].shape[1]
    wide = [h[...].astype(F32) for h in hid]
    square = sum(jnp.sum(h * h, axis=1, keepdims=True) for h in wide)
    scale = lax.rsqrt(square / (n * wc) + 1e-05)
    for k in range(n):
        at = pl.ds(pl.multiple_of((me[0] ^ k) * wc, wc), wc)
        out[:, at] = (wide[k] * scale * gain[:, at]).astype(BF)


def spread_kernel(n, m, me, expand, *refs):
    outs, scr = refs[-n - 1 : -1], refs[-1]
    out = refs[0][...]
    for k in range(1, m):
        out = out + refs[k][...].astype(F32)
    scr[...] = lax.dot_general(expand[...], out.astype(BF), TN, preferred_element_type=F32)
    size = outs[0].shape[0]
    for k in range(n):
        got = scr[pl.ds(pl.multiple_of((me[0] ^ k) * size, size), size), :]
        outs[k][...] = got.astype(outs[k].dtype)


def deal_kernel(n, m, me, *refs):
    keep, send, scr = refs[n:]
    total = refs[0][...]
    for k in range(1, n):
        total = total + refs[k][...].astype(F32)
    scr[...] = total
    rm = keep.shape[0] // m
    for q in range(2 * m):
        block = (me[1] ^ (q // 2)) * 2 + (me[2] ^ (q % 2))
        out = send if q % 2 else keep
        if rm % 8 == 0:
            got = scr[pl.ds(pl.multiple_of(block * rm, rm), rm), :]
        else:
            got = scr[:rm]
            for b in range(1, 2 * m):
                got = jnp.where(block == b, scr[b * rm : (b + 1) * rm], got)
        out[(q // 2) * rm : (q // 2 + 1) * rm, :] = got.astype(BF)


def pair_kernel(m, keep, got, *outs):
    rm = outs[0].shape[0]
    pc = keep.shape[1]
    for k in range(m):
        outs[k][:, :pc] = keep[k * rm : (k + 1) * rm]
        outs[k][:, pc:] = got[k * rm : (k + 1) * rm]


def hold_kernel(*refs):
    pass


def small(kern, name, outs, args, deps=(), scr=()):
    vm = pl.BlockSpec(memory_space=pltpu.VMEM)
    sm = pl.BlockSpec(memory_space=pltpu.SMEM)
    count = len(args)

    def run(*refs):
        kern(*refs[:count], *refs[count + len(deps) :])

    specs = [sm if a.dtype == jnp.int32 and a.ndim == 1 else vm for a in args]
    return pl.pallas_call(
        run,
        in_specs=specs + [pl.BlockSpec(memory_space=pl.ANY)] * len(deps),
        out_specs=[vm] * len(outs),
        out_shape=[jax.ShapeDtypeStruct(*o) for o in outs],
        scratch_shapes=list(scr),
        compiler_params=params(8),
        cost_estimate=cost(1e5, 1 << 12),
        name=name,
    )(*args, *deps)


def place_kernel(n, states, me, rr, *refs):
    srcs, (out, token, buf, sem) = refs[:n], refs[-4:]
    token[...] = jnp.zeros_like(token)
    i, last = pl.program_id(0), pl.num_programs(0) - 1
    slot = lax.rem(i, 2)

    def copies(step, where):
        return [
            pltpu.make_async_copy(buf.at[where, k], out.at[rr[0, me[0] ^ k, step]], sem.at[where, k])
            for k in range(n)
        ]

    @pl.when(i >= 2)
    def _():
        for copy in copies(i - 2, slot):
            copy.wait()

    for k in range(n):
        buf[slot, k] = srcs[k][...].astype(F32)
    for copy in copies(i, slot):
        copy.start()

    @pl.when(i == last)
    def _():
        for copy in copies(i - 1, 1 - slot):
            copy.wait()
        for copy in copies(i, slot):
            copy.wait()


def place(n, per, rows, states, me, rr, srcs, dep):
    ch = srcs[0].shape[1]
    return pl.pallas_call(
        functools.partial(place_kernel, n, states),
        grid_spec=pltpu.PrefetchScalarGridSpec(
            num_scalar_prefetch=2,
            grid=(per,),
            in_specs=[pl.BlockSpec((states, ch), lambda i, *_: (i, 0))] * n
            + [pl.BlockSpec(memory_space=pl.ANY)],
            out_specs=[
                pl.BlockSpec(memory_space=pl.ANY),
                pl.BlockSpec((8, 128), lambda i, *_: (0, 0)),
            ],
            scratch_shapes=[
                pltpu.VMEM((2, n, states, ch), F32),
                pltpu.SemaphoreType.DMA((2, n)),
            ],
        ),
        out_shape=[
            jax.ShapeDtypeStruct((rows, states, ch), F32),
            jax.ShapeDtypeStruct((8, 128), F32),
        ],
        compiler_params=params(8),
        cost_estimate=cost(1e5, 1 << 12),
        name="place",
    )(me, rr, *srcs, dep)


def tail_kernel(n, per, taps, me, rr, x, *refs):
    tails, (out, token) = refs[:n], refs[-2:]
    token[...] = jnp.zeros_like(token)
    steps = x.shape[0]
    keep = taps - steps
    for t in range(steps):
        out[keep + t] = x[t].astype(F32)
    for k in range(n):
        block = tails[k][...].astype(F32)
        for j in range(keep):
            for i in range(per):
                q = j * per + i
                out[j, pl.ds(rr[0, me[0] ^ k, i], 1), :] = block[q : q + 1, :]


def final_kernel(n, m, me, *refs):
    hid = refs[:n]
    parts = refs[n : n + m]
    out, acc = refs[-2:]
    wc = hid[0].shape[1]
    for k in range(n):
        acc[:, pl.ds(pl.multiple_of((me[0] ^ k) * wc, wc), wc)] = hid[k][...].astype(F32)
    pc = parts[0].shape[1] // 2
    for q in range(2 * m):
        zs, h = me[1] ^ (q // 2), q % 2
        where = pl.ds(pl.multiple_of(((me[2] ^ h) * m + zs) * pc, pc), pc)
        got = parts[q // 2][:, h * pc : (h + 1) * pc].astype(F32)
        acc[:, where] = acc[:, where] + got
    out[...] = acc[...].astype(BF)


def body(
    conv_cache,
    state_cache,
    send_slot,
    recv_row,
    prefix_length,
    x_input,
    z_input,
    dt_input,
    b_input,
    c_input,
    conv_weight,
    conv_bias,
    dt_bias,
    decay_rate,
    skip_gain,
    out_weight,
    norm_gain,
    route_ids,
    route_weight,
    expert_slots,
    gate_weight,
    up_weight,
    down_weight,
):
    n = lax.axis_size("dp")
    m = lax.axis_size("z")
    d, zz, cc = lax.axis_index("dp"), lax.axis_index("z"), lax.axis_index("core")
    me = jnp.stack([d, zz, cc]).astype(jnp.int32)
    steps, rows, ch = x_input.shape
    per = rows // n
    taps = conv_cache.shape[1]
    states = state_cache.shape[1]
    total = steps * n * rows
    cap = total // 4
    pe = cap // (2 * m)
    rm = total // (n * 2 * m)
    width = gate_weight.shape[1]
    wc = out_weight.shape[1]
    dm = n * wc
    rr, ss = recv_row, send_slot
    vm = pl.BlockSpec(memory_space=pltpu.VMEM)
    sm = pl.BlockSpec(memory_space=pltpu.SMEM)

    in_hbm = functools.partial(pltpu.with_memory_space_constraint, memory_space=pltpu.HBM)

    def whole(a):
        return pl.BlockSpec(a.shape, lambda g: (0,) * a.ndim)

    src = (
        x_input,
        z_input,
        dt_input,
        jnp.transpose(b_input, (0, 2, 1)),
        jnp.transpose(c_input, (0, 2, 1)),
        prefix_length.reshape(1, rows),
    )
    src = [in_hbm(a) for a in src]
    packed = jax.ShapeDtypeStruct((per, 3 * steps * ch + META), BF)
    payload = pl.pallas_call(
        functools.partial(pack_kernel, n, per),
        grid=(1,),
        in_specs=[sm, sm] + [whole(a) for a in src],
        out_specs=[whole(packed)] * n,
        out_shape=[packed] * n,
        scratch_shapes=[pltpu.VMEM((128, rows), F32)],
        compiler_params=params(12),
        cost_estimate=cost(1e6, 2 << 20),
        name="pack",
    )(me, recv_row, *src)
    payload = [payload[0]] + [trade(payload[k], "dp", n, k) for k in range(1, n)]
    par = jnp.concatenate(
        [conv_weight, conv_bias[None], dt_bias[None], skip_gain[None], jnp.zeros((1, ch), F32)], 0
    )
    conv = jnp.transpose(conv_cache, (1, 0, 2))
    fixed = (par, decay_rate, conv, state_cache)
    hbm = pl.BlockSpec(memory_space=pltpu.HBM)
    fixed = pl.pallas_call(
        functools.partial(fetch_kernel, len(fixed)),
        in_specs=[hbm] * len(fixed) + [pl.BlockSpec(memory_space=pl.ANY)],
        out_specs=[vm] * len(fixed),
        out_shape=[pltpu.VMEM(a.shape, a.dtype) for a in fixed],
        scratch_shapes=[pltpu.SemaphoreType.DMA((len(fixed),))],
        compiler_params=params(1),
        cost_estimate=cost(1e5, 1 << 12),
        name="fetch",
    )(*[in_hbm(a) for a in fixed], payload[0])
    y_first, own_kept = ssm(0, per, steps, me, ss, payload[:1], *fixed)
    y_own, *kept = ssm(1, per, steps, me, ss, [y_first] + payload[1:], *fixed)
    kept = [own_kept] + kept
    ys = [y_own] + [trade(y_own, "dp", n, k) for k in range(1, n)]

    n_slot, n_own = 2 * m * n * pe, 2 * m * n * rm
    ids_t = route_ids.reshape(total, -1).T
    wts_t = route_weight.reshape(total, -1).T
    meta_at = 3 * steps * ch // 128
    sel_slot, sel_own, share, expand = pl.pallas_call(
        functools.partial(select_kernel, n, m, per, steps, rows, rm, pe, width),
        grid=(1,),
        in_specs=[sm, sm]
        + [pl.BlockSpec(ids_t.shape, lambda g: (0, 0))] * 2
        + [pl.BlockSpec((per, 128), lambda g: (0, meta_at))] * n,
        out_specs=[
            pl.BlockSpec((n_slot, total), lambda g: (0, 0)),
            pl.BlockSpec((n_own, total), lambda g: (0, 0)),
            pl.BlockSpec((cap, 128), lambda g: (0, 0)),
            pl.BlockSpec((cap, total), lambda g: (0, 0)),
        ],
        out_shape=[
            jax.ShapeDtypeStruct((n_slot, total), BF),
            jax.ShapeDtypeStruct((n_own, total), BF),
            jax.ShapeDtypeStruct((cap, 128), F32),
            jax.ShapeDtypeStruct((cap, total), BF),
        ],
        compiler_params=params(10),
        cost_estimate=cost(1e7, 1 << 20),
        name="select",
    )(me, expert_slots, ids_t, wts_t, *payload)

    width = gate_weight.shape[1]
    chunks = 8
    gate_here, loaded = pl.pallas_call(
        functools.partial(load_kernel, chunks),
        in_specs=[pl.BlockSpec(memory_space=pltpu.HBM), pl.BlockSpec(memory_space=pl.ANY)],
        out_specs=[vm, vm],
        out_shape=[pltpu.VMEM(gate_weight.shape, BF), jax.ShapeDtypeStruct((8, 128), F32)],
        scratch_shapes=[pltpu.SemaphoreType.DMA((chunks,))],
        compiler_params=params(1),
        cost_estimate=cost(1e5, 1 << 12),
        name="load",
    )(in_hbm(gate_weight), y_own)
    anyspace = pl.BlockSpec(memory_space=pl.ANY)

    def add_core(keep, send, each, name, dep=()):
        got = trade(send, "core", 2, 1)
        shape = (n * each, wc)
        outs = [(shape, F32)] + [(shape, BF)] * (m - 1)
        return small(functools.partial(pair_rows_kernel, m), name, outs, (keep, got), dep)

    def send_z(parts):
        return [parts[0]] + [trade(parts[k], "z", m, k) for k in range(1, m)]

    def add_z(got, each, name, dep=()):
        outs = [((each, wc), BF)] * n
        out = small(functools.partial(sum_rows_kernel, len(got), n), name, outs, got, dep)
        return [out[0]] + [trade(out[k], "dp", n, k) for k in range(1, n)]

    keep_slot, send_slot_rows, keep_own, send_own = project(
        n, ys, sel_slot, sel_own, out_weight, loaded
    )
    parts = add_core(keep_slot, send_slot_rows, pe, "core_slot")
    slot_z = send_z(parts)
    hid = add_z(slot_z, pe, "z_slot")
    [normed] = small(
        functools.partial(norm_kernel, n),
        "norm",
        [((pe, dm), BF)],
        (me, norm_gain.reshape(1, dm), *hid),
    )
    near = [normed] + [trade(normed, "z", m, k) for k in range(1, m)]
    xs = []
    for piece in near:
        xs += [piece, trade(piece, "core", 2, 1)]
    size = m * n * rm // 2
    halves = [((size, wc), F32), ((size, wc), BF)]
    own_keep, own_send = small(
        functools.partial(pair_rows_kernel, 2),
        "core_own",
        halves,
        (keep_own, trade(send_own, "core", 2, 1)),
        (near[1],),
    )
    held = pl.pallas_call(
        hold_kernel,
        in_specs=[anyspace] * n,
        out_specs=[anyspace] * (n - 1),
        out_shape=[jax.ShapeDtypeStruct(k.shape, k.dtype) for k in kept[1:]],
        input_output_aliases={k: k for k in range(n - 1)},
        compiler_params=params(1),
        name="hold",
    )(*kept[1:], near[1])
    back = [kept[0]] + [trade(held[k - 1], "dp", n, k) for k in range(1, n)]

    half = dm // 2
    pc = half // m
    ub = 256 if width % 256 == 0 else 128
    act = pl.pallas_call(
        functools.partial(gate_kernel, m),
        in_specs=[sm] + [vm] * (2 * m + 2) + [pl.BlockSpec(memory_space=pltpu.HBM)],
        out_specs=vm,
        out_shape=jax.ShapeDtypeStruct((cap, width), BF),
        scratch_shapes=[
            pltpu.VMEM((cap, dm), BF),
            pltpu.VMEM((2, dm, ub), BF),
            pltpu.SemaphoreType.DMA((2,)),
        ],
        compiler_params=params(14),
        cost_estimate=cost(4 * cap * dm * width, 4 * dm * width),
        name="gate",
    )(me, *xs, share, gate_here, in_hbm(up_weight))
    k = m // 2
    while k > 1:
        size //= 2
        own_keep, own_send = small(
            functools.partial(pair_rows_kernel, 2),
            f"half{k}",
            [((size, wc), F32), ((size, wc), BF)],
            (own_keep, trade(own_send, "z", m, k)),
        )
        k //= 2
    own_z = [own_keep, trade(own_send, "z", m, 1)]
    deps = [own_send] + back[1:]
    send, keep = pl.pallas_call(
        functools.partial(down_kernel, m, len(deps)),
        in_specs=[sm, vm, pl.BlockSpec(memory_space=pltpu.HBM)] + [anyspace] * len(deps),
        out_specs=[vm] * 2,
        out_shape=[jax.ShapeDtypeStruct((cap, half), BF)] * 2,
        scratch_shapes=[pltpu.VMEM((6, width, pc // 2), BF), pltpu.SemaphoreType.DMA((6,))],
        compiler_params=params(14),
        cost_estimate=cost(2 * cap * dm * width, 2 * dm * width),
        name="down",
    )(me, act, in_hbm(down_weight), *deps)

    got = trade(send, "core", 2, 1)
    outs = [((cap, pc), F32)] + [((cap, pc), BF)] * (m - 1)
    cols = small(functools.partial(pair_cols_kernel, m), "core_out", outs, (keep, got))
    moved = [cols[0]] + [trade(cols[k], "z", m, k) for k in range(1, m)]

    own = add_z(own_z, rm, "z_own", (cols[1],))
    low = kept[0].shape[0] - per * states
    tail_at = per * states // low
    new_tail, tailed = pl.pallas_call(
        functools.partial(tail_kernel, n, per, taps),
        grid=(1,),
        in_specs=[sm, sm, pl.BlockSpec(x_input.shape, lambda g: (0, 0, 0))]
        + [pl.BlockSpec((low, ch), lambda g: (tail_at, 0))] * n
        + [anyspace],
        out_specs=[
            pl.BlockSpec((taps, rows, ch), lambda g: (0, 0, 0)),
            pl.BlockSpec((8, 128), lambda g: (0, 0)),
        ],
        out_shape=[
            jax.ShapeDtypeStruct((taps, rows, ch), F32),
            jax.ShapeDtypeStruct((8, 128), F32),
        ],
        compiler_params=params(8),
        cost_estimate=cost(1e5, 1 << 12),
        name="tail",
    )(me, rr, x_input, *back, cols[1])
    share_rows = total // n
    outs = [((share_rows, pc), F32)] + [((share_rows, pc), BF)] * (n - 1)
    rows_out = small(
        functools.partial(spread_kernel, n, m),
        "spread",
        outs,
        (me, expand, *moved),
        (tailed, *own[1:]),
        [pltpu.VMEM((total, pc), F32)],
    )
    new_state, placed = place(n, per, rows, states, me, rr, back, rows_out[1])

    mine = [rows_out[0]] + [trade(rows_out[k], "dp", n, k) for k in range(1, n)]
    deal_keep, deal_send = small(
        functools.partial(deal_kernel, n, m),
        "deal",
        [((m * rm, pc), BF)] * 2,
        (me, *mine),
        (placed,),
        [pltpu.VMEM((share_rows, pc), F32)],
    )
    pieces = small(
        functools.partial(pair_kernel, m),
        "pair",
        [((rm, 2 * pc), BF)] * m,
        (deal_keep, trade(deal_send, "core", 2, 1)),
    )
    pieces = send_z(pieces)
    [mixed] = small(
        functools.partial(final_kernel, n, m),
        "final",
        [((rm, dm), BF)],
        (me, *own, *pieces),
        (),
        [pltpu.VMEM((rm, dm), F32)],
    )
    return (mixed, new_state, jnp.transpose(new_tail, (1, 0, 2)))


def solution(mesh):
    n = mesh.shape["dp"]
    m = mesh.shape["expert"] // 2
    split = Mesh(mesh.devices.reshape(n, m, 2), ("dp", "z", "core"))
    e = ("z", "core")
    de = ("dp", "z", "core")
    in_specs = (
        P("dp", None, e),
        P("dp", None, e),
        P(),
        P("dp", None, None),
        P("dp"),
        P(None, "dp", e),
        P(None, "dp", e),
        P(None, "dp", e),
        P(None, "dp", None),
        P(None, "dp", None),
        P(None, e),
        P(e),
        P(e),
        P(None, e),
        P(e),
        P(e, "dp"),
        P(),
        P(),
        P(),
        P(),
        P(None, de),
        P(None, de),
        P(de, None),
    )
    out_specs = (P(de, None), P("dp", None, e), P("dp", None, e))
    return jax.shard_map(body, mesh=split, in_specs=in_specs, out_specs=out_specs, check_vma=False)
```

```python
import functools

import jax
import jax.numpy as jnp
from jax import lax
from jax.experimental import pallas as pl
from jax.experimental.pallas import tpu as pltpu
from jax.sharding import Mesh
from jax.sharding import PartitionSpec as P

FFW = 12288
BF = jnp.bfloat16
F32 = jnp.float32
META = 256
TABLE = 96
PREFIX = 64
NT = (((1,), (1,)), ((), ()))
TN = (((0,), (0,)), ((), ()))


def cost(flops, moved):
    return pl.CostEstimate(flops=int(flops), bytes_accessed=int(moved), transcendentals=0)


def params(limit):
    return pltpu.CompilerParams(vmem_limit_bytes=limit << 20)


def iota(shape, dim):
    return lax.broadcasted_iota(jnp.int32, shape, dim)


def trade(piece, axis, size, k):
    return lax.ppermute(piece, axis, [(i, i ^ k) for i in range(size)])


def pack_kernel(n, per, me, rr, x, z, dt, b, c, prefix, *rest):
    outs, m_scr = rest[:n], rest[n]
    steps, rows, ch = x.shape
    states = b.shape[1]
    m_scr[...] = jnp.zeros_like(m_scr)
    for t in range(steps):
        m_scr[2 * t * states : (2 * t + 1) * states, :] = b[t]
        m_scr[(2 * t + 1) * states : (2 * t + 2) * states, :] = c[t]
    m_scr[PREFIX : PREFIX + 1, :] = prefix[...].astype(F32)
    rowcol = jnp.zeros((n * per, 1), jnp.int32)
    table = jnp.zeros((1, 128), F32)
    sub = iota((n * per, 1), 0)
    lane = iota((1, 128), 1)
    for k in range(n):
        for i in range(per):
            rowcol = jnp.where(sub == k * per + i, rr[0, me[0] ^ k, i], rowcol)
            q = k * per + i
            table = jnp.where(lane == TABLE + q, rr[0, k, i].astype(F32), table)
    hot = rowcol == iota((n * per, rows), 1)
    hot_b = hot.astype(BF)
    for a, src in enumerate((x, z, dt)):
        for t in range(steps):
            got = jnp.dot(hot_b, src[t], preferred_element_type=F32).astype(BF)
            at = (a * steps + t) * ch
            for k in range(n):
                outs[k][:, at : at + ch] = got[k * per : (k + 1) * per]
    meta = lax.dot_general(
        hot.astype(F32), m_scr[...], NT, precision=lax.Precision.HIGHEST, preferred_element_type=F32
    )
    meta = meta + table
    hi = meta.astype(BF)
    lo = (meta - hi.astype(F32)).astype(BF)
    at = 3 * steps * ch
    for k in range(n):
        outs[k][:, at : at + 128] = hi[k * per : (k + 1) * per]
        outs[k][:, at + 128 : at + 256] = lo[k * per : (k + 1) * per]


def ssm_kernel(first, groups, per, steps, me, ss, *refs):
    if first:
        y_first, refs = refs[0], refs[1:]
    loads = refs[:groups]
    par, decay, conv, state, y_out = refs[groups : groups + 5]
    st_outs = refs[groups + 5 : 2 * groups + 5]
    y_scr, tail_scr, bc_scr, du_scr = refs[2 * groups + 5 :]
    taps, _, ch = conv.shape
    states = decay.shape[0]
    cb = y_scr.shape[2]
    lb = min(256, cb)
    low = st_outs[0].shape[0] - per * states
    done = 0
    if first:
        done = y_first.shape[0]
        y_out[:done, :] = y_first[...]
    at = 3 * steps * ch
    masks = []
    for q in range(groups):
        val = loads[q][:, at : at + 128].astype(F32) + loads[q][:, at + 128 : at + 256].astype(F32)
        full = jnp.concatenate([val, jnp.zeros((128 - per, 128), F32)], axis=0)
        bc_scr[q] = jnp.transpose(full)
        prefix = val[:, PREFIX : PREFIX + 1]
        masks.append([(prefix >= float(taps - j)).astype(F32) for j in range(taps)])

    @pl.loop(0, ch // cb)
    def _(g):
        base = pl.multiple_of(g * cb, cb)
        wide = pl.ds(base, cb)
        for q in range(groups):
            slots = [ss[me[0], me[0] ^ (q + first), i] for i in range(per)]

            def load(a):
                return loads[q][:, pl.ds(pl.multiple_of(a * ch + base, cb), cb)].astype(F32)

            for j in range(taps):
                for i in range(per):
                    tail_scr[j, i : i + 1, :] = conv[j, pl.ds(slots[i], 1), wide]
            window = [tail_scr[j] * masks[q][j] for j in range(taps)]
            skips, gates = [], []
            for t in range(steps):
                window.append(load(t))
                acc = window[t] * par[0:1, wide]
                for j in range(1, taps + 1):
                    acc = acc + window[t + j] * par[j : j + 1, wide]
                acc = acc + par[taps + 1 : taps + 2, wide]
                xc = acc * jax.nn.sigmoid(acc)
                raw = load(2 * steps + t) + par[taps + 2 : taps + 3, wide]
                delta = jnp.maximum(raw, 0.0) + jnp.log1p(jnp.exp(-jnp.abs(raw)))
                zt = load(steps + t)
                du_scr[2 * t] = delta * -1.4426950408889634
                du_scr[2 * t + 1] = delta * xc
                skips.append(par[taps + 3 : taps + 4, wide] * xc)
                gates.append(zt * jax.nn.sigmoid(zt))
            kept = window[steps:taps]
            kept.append(jnp.zeros((low - per * len(kept), cb), F32))
            kept = jnp.concatenate(kept, axis=0)
            st_outs[q][per * states :, wide] = kept.astype(st_outs[q].dtype)
            for i in range(per):
                cols = []
                for k in range(2 * steps):
                    col = bc_scr[q, k * states : (k + 1) * states, i : i + 1]
                    cols.append(jnp.broadcast_to(col, (states, lb)))
                for l in range(cb // lb):
                    here = slice(l * lb, (l + 1) * lb)
                    there = pl.ds(pl.multiple_of(base + l * lb, lb), lb)
                    st = state[slots[i], :, there]
                    for t in range(steps):
                        dl = du_scr[2 * t, i : i + 1, here]
                        ul = du_scr[2 * t + 1, i : i + 1, here]
                        st = jnp.exp2(dl * decay[:, there]) * st + ul * cols[2 * t]
                        y_scr[t, i : i + 1, here] = jnp.sum(
                            cols[2 * t + 1] * st, axis=0, keepdims=True
                        )
                    st_outs[q][i * states : (i + 1) * states, there] = st.astype(st_outs[q].dtype)
            for t in range(steps):
                row = done + (q * steps + t) * per
                y_out[row : row + per, wide] = ((y_scr[t] + skips[t]) * gates[t]).astype(BF)


def ssm(first, per, steps, me, ss, payloads, par, decay, conv, state):
    groups = len(payloads)
    states, ch = decay.shape
    cb = ch // 4
    taps = conv.shape[0]
    low = -(-(taps - steps) * per // 16) * 16
    vm = pl.BlockSpec(memory_space=pltpu.VMEM)
    sm = pl.BlockSpec(memory_space=pltpu.SMEM)
    args = list(payloads) + [par, decay, conv, state]
    groups -= first
    return pl.pallas_call(
        functools.partial(ssm_kernel, first, groups, per, steps),
        in_specs=[sm, sm] + [vm] * len(args),
        out_specs=[vm] * (1 + groups),
        out_shape=[jax.ShapeDtypeStruct(((first + groups) * steps * per, ch), BF)]
        + [
            jax.ShapeDtypeStruct((per * states + low, ch), BF if first else F32)
            for q in range(groups)
        ],
        scratch_shapes=[
            pltpu.VMEM((steps, per, cb), F32),
            pltpu.VMEM((taps, per, cb), F32),
            pltpu.VMEM((groups, 128, 128), F32),
            pltpu.VMEM((2 * steps, per, cb), F32),
        ],
        compiler_params=params(4),
        cost_estimate=cost(3e6 * groups, groups * 3 << 20),
        name=f"ssm{first}",
    )(me, ss, *args)


def select_kernel(n, m, per, steps, rows, rm, pe, width, me, es, ids, wts, *refs):
    tables = refs[:n]
    sel_slot, sel_own, share, expand = refs[n:]
    cores = m * 2
    d, zz, cc = me[0], me[1], me[2]
    total = steps * n * rows
    choices = ids.shape[0]
    sub8 = iota((8, total), 0)
    match = jnp.zeros((8, total), F32)
    own_share = jnp.zeros((1, total), F32)
    hits = []
    for kd in range(n):
        eid = es[((d ^ kd) * (cores * width)) // FFW]
        hit = jnp.zeros((1, total), F32)
        for q in range(choices):
            same = ids[q : q + 1, :] == eid
            hit = jnp.where(same, 1.0, hit)
            if kd == 0:
                own_share = own_share + jnp.where(same, wts[q : q + 1, :], 0.0)
        hits.append(hit)
        match = jnp.where(sub8 == kd, hit, match)
    before = (iota((total, total), 0) < iota((total, total), 1)).astype(BF)
    pos = jnp.dot(match.astype(BF), before, preferred_element_type=F32)
    pos = jnp.where(match > 0.0, pos, -1.0)
    col = iota((pe, 1), 0)
    parts, owns = [], []
    for h in range(2):
        for kz in range(m):
            first = ((zz ^ kz) * 2 + (cc ^ h)) * pe
            want = (col + first).astype(F32)
            for kd in range(n):
                parts.append((pos[kd : kd + 1, :] == want).astype(BF))
        row = iota((m * n * rm, 1), 0)
        kz_v = row // (n * rm)
        kd_v = (row // rm) % n
        true = ((d ^ kd_v) * cores + (zz ^ kz_v) * 2 + (cc ^ h)) * rm + row % rm
        owns.append((true == iota((m * n * rm, total), 1)).astype(BF))
    sel_true = jnp.concatenate(parts + owns, axis=0)
    j = iota((total, 1), 0)
    ko = j // (n * steps * per)
    kd = (j // (steps * per)) % n
    tab = jnp.zeros((8, 128), F32)
    for q in range(n):
        tab = jnp.where(iota((8, 128), 0) == q, tables[q][0:1, :].astype(F32), tab)
    pick = (iota((total, 8), 1) == (ko ^ kd)).astype(BF)
    tj = jnp.dot(pick, tab.astype(BF), preferred_element_type=F32)
    lane = TABLE + (d ^ ko) * per + j % per
    local = jnp.sum(jnp.where(iota((total, 128), 1) == lane, tj, 0.0), axis=1, keepdims=True)
    true = ((j // per) % steps) * (n * rows) + (d ^ ko ^ kd) * rows + local.astype(jnp.int32)
    perm = (true == iota((total, total), 1)).astype(BF)
    sel = lax.dot_general(sel_true, perm, NT, preferred_element_type=F32).astype(BF)
    count = sel_slot.shape[0]
    sel_slot[...] = sel[:count]
    sel_own[...] = sel[count:]
    hot = pos[0:1, :] == iota((cores * pe, 1), 0).astype(F32)
    expand[...] = hot.astype(BF)
    mine = jnp.sum(jnp.where(hot, own_share, 0.0), axis=1, keepdims=True)
    share[...] = jnp.broadcast_to(mine, share.shape)


def project_kernel(n, *refs):
    ys = refs[:n]
    sel_slot, sel_own, w = refs[n : n + 3]
    *outs, y_all, y_sel = refs[-6:]
    size = ys[0].shape[0]
    for q in range(n):
        y_all[q * size : (q + 1) * size, :] = ys[q][...]
    at = 0
    for sel in (sel_slot, sel_own):
        got = jnp.dot(sel[...], y_all[...], preferred_element_type=F32).astype(BF)
        y_sel[at : at + got.shape[0], :] = got
        at += got.shape[0]
    wb = min(1024, w.shape[1])

    @pl.loop(0, w.shape[1] // wb)
    def _(g):
        at = pl.ds(pl.multiple_of(g * wb, wb), wb)
        out = jnp.dot(y_sel[...], w[:, at], preferred_element_type=F32).astype(BF)
        row = 0
        for part in outs:
            part[:, at] = out[row : row + part.shape[0]]
            row += part.shape[0]


def project(n, ys, sel_slot, sel_own, w, dep):
    vm = pl.BlockSpec(memory_space=pltpu.VMEM)
    slot, total = sel_slot.shape
    own = sel_own.shape[0]
    ch, wc = w.shape
    return pl.pallas_call(
        functools.partial(project_kernel, n),
        in_specs=[vm] * (n + 3) + [pl.BlockSpec(memory_space=pl.ANY)],
        out_specs=[vm] * 4,
        out_shape=[jax.ShapeDtypeStruct((slot // 2, wc), BF)] * 2
        + [jax.ShapeDtypeStruct((own // 2, wc), BF)] * 2,
        scratch_shapes=[pltpu.VMEM((total, ch), BF), pltpu.VMEM((slot + own, ch), BF)],
        compiler_params=params(10),
        cost_estimate=cost(1e5, 1 << 12),
        name="project",
    )(*ys, sel_slot, sel_own, w, dep)


def load_kernel(chunks, w, *refs):
    out, token, sem = refs[-3:]
    token[...] = jnp.zeros_like(token)
    size = w.shape[0] // chunks
    copies = [
        pltpu.make_async_copy(
            w.at[pl.ds(q * size, size)], out.at[pl.ds(q * size, size)], sem.at[q]
        )
        for q in range(chunks)
    ]
    for copy in copies:
        copy.start()
    for copy in copies:
        copy.wait()


def fetch_kernel(count, *refs):
    srcs, outs, sem = refs[:count], refs[-count - 1 : -1], refs[-1]
    copies = [pltpu.make_async_copy(srcs[q], outs[q], sem.at[q]) for q in range(count)]
    for copy in copies:
        copy.start()
    for copy in copies:
        copy.wait()


def gate_kernel(m, me, *refs):
    pieces = 2 * m
    xs = refs[:pieces]
    share, gw, uw, act, x_scr, ubuf, usem = refs[pieces:]
    pe = xs[0].shape[0]
    ub, deep = ubuf.shape[2], ubuf.shape[0]
    nu = gw.shape[1] // ub

    def up_copy(j):
        return pltpu.make_async_copy(
            uw.at[:, pl.ds(pl.multiple_of(j * ub, ub), ub)],
            ubuf.at[lax.rem(j, deep)],
            usem.at[lax.rem(j, deep)],
        )

    for j in range(min(deep, nu)):
        up_copy(j).start()
    first = me[2] == 0
    for kz in range(m):
        own, other = xs[2 * kz][...].astype(F32), xs[2 * kz + 1][...].astype(F32)
        pair = jnp.concatenate(
            [jnp.where(first, own, other), jnp.where(first, other, own)], axis=0
        ).astype(BF)
        at = pl.multiple_of((me[1] ^ kz) * (2 * pe), 2 * pe)
        x_scr[pl.ds(at, 2 * pe), :] = pair

    @pl.loop(0, nu)
    def _(j):
        at = pl.ds(pl.multiple_of(j * ub, ub), ub)
        gated = jnp.dot(x_scr[...], gw[:, at], preferred_element_type=F32)
        up_copy(j).wait()
        upped = jnp.dot(x_scr[...], ubuf[lax.rem(j, deep)], preferred_element_type=F32)

        @pl.when(j + deep < nu)
        def _():
            up_copy(j + deep).start()

        act[:, at] = (gated * jax.nn.sigmoid(gated) * upped * share[:, 0:1]).astype(BF)


def down_kernel(m, deps, me, act, dw, *refs):
    send, keep, dbuf, dsem = refs[deps:]
    pc, deep = dbuf.shape[2], dbuf.shape[0]
    nh = send.shape[1] // pc
    cut = nh // m
    nd = 2 * nh

    def down_copy(i):
        h, j = jnp.where(i < nh, 1, 0), lax.rem(i, nh)
        block = ((me[2] ^ h) * m + (me[1] ^ lax.div(j, cut))) * cut + lax.rem(j, cut)
        return pltpu.make_async_copy(
            dw.at[:, pl.ds(pl.multiple_of(block * pc, pc), pc)],
            dbuf.at[lax.rem(i, deep)],
            dsem.at[lax.rem(i, deep)],
        )

    for i in range(min(deep, nd)):
        down_copy(i).start()

    @pl.loop(0, nd)
    def _(i):
        down_copy(i).wait()
        out = jnp.dot(act[...], dbuf[lax.rem(i, deep)], preferred_element_type=F32).astype(BF)
        at = pl.ds(pl.multiple_of(lax.rem(i, nh) * pc, pc), pc)

        @pl.when(i < nh)
        def _():
            send[:, at] = out

        @pl.when(i >= nh)
        def _():
            keep[:, at] = out

        @pl.when(i + deep < nd)
        def _():
            down_copy(i + deep).start()


def pair_rows_kernel(count, keep, got, *refs):
    outs = refs[-count:]
    size = outs[0].shape[0]
    for k in range(count):
        at = slice(k * size, (k + 1) * size)
        both = keep[at].astype(F32) + got[at].astype(F32)
        outs[k][...] = both.astype(outs[k].dtype)


def pair_cols_kernel(count, keep, got, *refs):
    outs = refs[-count:]
    size = outs[0].shape[1]
    for k in range(count):
        at = slice(k * size, (k + 1) * size)
        both = keep[:, at].astype(F32) + got[:, at].astype(F32)
        outs[k][...] = both.astype(outs[k].dtype)


def sum_rows_kernel(count, parts, *refs):
    outs = refs[-parts:]
    size = outs[0].shape[0]
    total = refs[0][...]
    for k in range(1, count):
        total = total + refs[k][...].astype(F32)
    for k in range(parts):
        outs[k][...] = total[k * size : (k + 1) * size].astype(BF)


def norm_kernel(n, me, gain, *refs):
    hid, out = refs[:n], refs[n]
    wc = hid[0].shape[1]
    wide = [h[...].astype(F32) for h in hid]
    square = sum(jnp.sum(h * h, axis=1, keepdims=True) for h in wide)
    scale = lax.rsqrt(square / (n * wc) + 1e-05)
    for k in range(n):
        at = pl.ds(pl.multiple_of((me[0] ^ k) * wc, wc), wc)
        out[:, at] = (wide[k] * scale * gain[:, at]).astype(BF)


def spread_kernel(n, m, me, expand, *refs):
    outs, scr = refs[-n - 1 : -1], refs[-1]
    out = refs[0][...]
    for k in range(1, m):
        out = out + refs[k][...].astype(F32)
    scr[...] = lax.dot_general(expand[...], out.astype(BF), TN, preferred_element_type=F32)
    size = outs[0].shape[0]
    for k in range(n):
        got = scr[pl.ds(pl.multiple_of((me[0] ^ k) * size, size), size), :]
        outs[k][...] = got.astype(outs[k].dtype)


def deal_kernel(n, m, me, *refs):
    keep, send, scr = refs[n:]
    total = refs[0][...]
    for k in range(1, n):
        total = total + refs[k][...].astype(F32)
    scr[...] = total
    rm = keep.shape[0] // m
    for q in range(2 * m):
        block = (me[1] ^ (q // 2)) * 2 + (me[2] ^ (q % 2))
        out = send if q % 2 else keep
        if rm % 8 == 0:
            got = scr[pl.ds(pl.multiple_of(block * rm, rm), rm), :]
        else:
            got = scr[:rm]
            for b in range(1, 2 * m):
                got = jnp.where(block == b, scr[b * rm : (b + 1) * rm], got)
        out[(q // 2) * rm : (q // 2 + 1) * rm, :] = got.astype(BF)


def pair_kernel(m, keep, got, *outs):
    rm = outs[0].shape[0]
    pc = keep.shape[1]
    for k in range(m):
        outs[k][:, :pc] = keep[k * rm : (k + 1) * rm]
        outs[k][:, pc:] = got[k * rm : (k + 1) * rm]


def hold_kernel(*refs):
    pass


def small(kern, name, outs, args, deps=(), scr=()):
    vm = pl.BlockSpec(memory_space=pltpu.VMEM)
    sm = pl.BlockSpec(memory_space=pltpu.SMEM)
    count = len(args)

    def run(*refs):
        kern(*refs[:count], *refs[count + len(deps) :])

    specs = [sm if a.dtype == jnp.int32 and a.ndim == 1 else vm for a in args]
    return pl.pallas_call(
        run,
        in_specs=specs + [pl.BlockSpec(memory_space=pl.ANY)] * len(deps),
        out_specs=[vm] * len(outs),
        out_shape=[jax.ShapeDtypeStruct(*o) for o in outs],
        scratch_shapes=list(scr),
        compiler_params=params(8),
        cost_estimate=cost(1e5, 1 << 12),
        name=name,
    )(*args, *deps)


def place_kernel(n, states, me, rr, *refs):
    srcs, (out, token, buf, sem) = refs[:n], refs[-4:]
    token[...] = jnp.zeros_like(token)
    i, last = pl.program_id(0), pl.num_programs(0) - 1
    slot = lax.rem(i, 2)

    def copies(step, where):
        return [
            pltpu.make_async_copy(buf.at[where, k], out.at[rr[0, me[0] ^ k, step]], sem.at[where, k])
            for k in range(n)
        ]

    @pl.when(i >= 2)
    def _():
        for copy in copies(i - 2, slot):
            copy.wait()

    for k in range(n):
        buf[slot, k] = srcs[k][...].astype(F32)
    for copy in copies(i, slot):
        copy.start()

    @pl.when(i == last)
    def _():
        for copy in copies(i - 1, 1 - slot):
            copy.wait()
        for copy in copies(i, slot):
            copy.wait()


def place(n, per, rows, states, me, rr, srcs, dep):
    ch = srcs[0].shape[1]
    return pl.pallas_call(
        functools.partial(place_kernel, n, states),
        grid_spec=pltpu.PrefetchScalarGridSpec(
            num_scalar_prefetch=2,
            grid=(per,),
            in_specs=[pl.BlockSpec((states, ch), lambda i, *_: (i, 0))] * n
            + [pl.BlockSpec(memory_space=pl.ANY)],
            out_specs=[
                pl.BlockSpec(memory_space=pl.ANY),
                pl.BlockSpec((8, 128), lambda i, *_: (0, 0)),
            ],
            scratch_shapes=[
                pltpu.VMEM((2, n, states, ch), F32),
                pltpu.SemaphoreType.DMA((2, n)),
            ],
        ),
        out_shape=[
            jax.ShapeDtypeStruct((rows, states, ch), F32),
            jax.ShapeDtypeStruct((8, 128), F32),
        ],
        compiler_params=params(8),
        cost_estimate=cost(1e5, 1 << 12),
        name="place",
    )(me, rr, *srcs, dep)


def tail_kernel(n, per, taps, me, rr, x, *refs):
    tails, (out, token) = refs[:n], refs[-2:]
    token[...] = jnp.zeros_like(token)
    steps = x.shape[0]
    keep = taps - steps
    for t in range(steps):
        out[keep + t] = x[t].astype(F32)
    for k in range(n):
        block = tails[k][...].astype(F32)
        for j in range(keep):
            for i in range(per):
                q = j * per + i
                out[j, pl.ds(rr[0, me[0] ^ k, i], 1), :] = block[q : q + 1, :]


def final_kernel(n, m, me, *refs):
    hid = refs[:n]
    parts = refs[n : n + m]
    out, acc = refs[-2:]
    wc = hid[0].shape[1]
    for k in range(n):
        acc[:, pl.ds(pl.multiple_of((me[0] ^ k) * wc, wc), wc)] = hid[k][...].astype(F32)
    pc = parts[0].shape[1] // 2
    for q in range(2 * m):
        zs, h = me[1] ^ (q // 2), q % 2
        where = pl.ds(pl.multiple_of(((me[2] ^ h) * m + zs) * pc, pc), pc)
        got = parts[q // 2][:, h * pc : (h + 1) * pc].astype(F32)
        acc[:, where] = acc[:, where] + got
    out[...] = acc[...].astype(BF)


def body(
    conv_cache,
    state_cache,
    send_slot,
    recv_row,
    prefix_length,
    x_input,
    z_input,
    dt_input,
    b_input,
    c_input,
    conv_weight,
    conv_bias,
    dt_bias,
    decay_rate,
    skip_gain,
    out_weight,
    norm_gain,
    route_ids,
    route_weight,
    expert_slots,
    gate_weight,
    up_weight,
    down_weight,
):
    n = lax.axis_size("dp")
    m = lax.axis_size("z")
    d, zz, cc = lax.axis_index("dp"), lax.axis_index("z"), lax.axis_index("core")
    me = jnp.stack([d, zz, cc]).astype(jnp.int32)
    steps, rows, ch = x_input.shape
    per = rows // n
    taps = conv_cache.shape[1]
    states = state_cache.shape[1]
    total = steps * n * rows
    cap = total // 4
    pe = cap // (2 * m)
    rm = total // (n * 2 * m)
    width = gate_weight.shape[1]
    wc = out_weight.shape[1]
    dm = n * wc
    rr, ss = recv_row, send_slot
    vm = pl.BlockSpec(memory_space=pltpu.VMEM)
    sm = pl.BlockSpec(memory_space=pltpu.SMEM)

    in_hbm = functools.partial(pltpu.with_memory_space_constraint, memory_space=pltpu.HBM)

    def whole(a):
        return pl.BlockSpec(a.shape, lambda g: (0,) * a.ndim)

    src = (
        x_input,
        z_input,
        dt_input,
        jnp.transpose(b_input, (0, 2, 1)),
        jnp.transpose(c_input, (0, 2, 1)),
        prefix_length.reshape(1, rows),
    )
    src = [in_hbm(a) for a in src]
    packed = jax.ShapeDtypeStruct((per, 3 * steps * ch + META), BF)
    payload = pl.pallas_call(
        functools.partial(pack_kernel, n, per),
        grid=(1,),
        in_specs=[sm, sm] + [whole(a) for a in src],
        out_specs=[whole(packed)] * n,
        out_shape=[packed] * n,
        scratch_shapes=[pltpu.VMEM((128, rows), F32)],
        compiler_params=params(12),
        cost_estimate=cost(1e6, 2 << 20),
        name="pack",
    )(me, recv_row, *src)
    payload = [payload[0]] + [trade(payload[k], "dp", n, k) for k in range(1, n)]
    par = jnp.concatenate(
        [conv_weight, conv_bias[None], dt_bias[None], skip_gain[None], jnp.zeros((1, ch), F32)], 0
    )
    conv = jnp.transpose(conv_cache, (1, 0, 2))
    fixed = (par, decay_rate, conv, state_cache)
    hbm = pl.BlockSpec(memory_space=pltpu.HBM)
    fixed = pl.pallas_call(
        functools.partial(fetch_kernel, len(fixed)),
        in_specs=[hbm] * len(fixed) + [pl.BlockSpec(memory_space=pl.ANY)],
        out_specs=[vm] * len(fixed),
        out_shape=[pltpu.VMEM(a.shape, a.dtype) for a in fixed],
        scratch_shapes=[pltpu.SemaphoreType.DMA((len(fixed),))],
        compiler_params=params(1),
        cost_estimate=cost(1e5, 1 << 12),
        name="fetch",
    )(*[in_hbm(a) for a in fixed], payload[0])
    y_first, own_kept = ssm(0, per, steps, me, ss, payload[:1], *fixed)
    y_own, *kept = ssm(1, per, steps, me, ss, [y_first] + payload[1:], *fixed)
    kept = [own_kept] + kept
    ys = [y_own] + [trade(y_own, "dp", n, k) for k in range(1, n)]

    n_slot, n_own = 2 * m * n * pe, 2 * m * n * rm
    ids_t = route_ids.reshape(total, -1).T
    wts_t = route_weight.reshape(total, -1).T
    meta_at = 3 * steps * ch // 128
    sel_slot, sel_own, share, expand = pl.pallas_call(
        functools.partial(select_kernel, n, m, per, steps, rows, rm, pe, width),
        grid=(1,),
        in_specs=[sm, sm]
        + [pl.BlockSpec(ids_t.shape, lambda g: (0, 0))] * 2
        + [pl.BlockSpec((per, 128), lambda g: (0, meta_at))] * n,
        out_specs=[
            pl.BlockSpec((n_slot, total), lambda g: (0, 0)),
            pl.BlockSpec((n_own, total), lambda g: (0, 0)),
            pl.BlockSpec((cap, 128), lambda g: (0, 0)),
            pl.BlockSpec((cap, total), lambda g: (0, 0)),
        ],
        out_shape=[
            jax.ShapeDtypeStruct((n_slot, total), BF),
            jax.ShapeDtypeStruct((n_own, total), BF),
            jax.ShapeDtypeStruct((cap, 128), F32),
            jax.ShapeDtypeStruct((cap, total), BF),
        ],
        compiler_params=params(10),
        cost_estimate=cost(1e7, 1 << 20),
        name="select",
    )(me, expert_slots, ids_t, wts_t, *payload)

    width = gate_weight.shape[1]
    chunks = 8
    gate_here, loaded = pl.pallas_call(
        functools.partial(load_kernel, chunks),
        in_specs=[pl.BlockSpec(memory_space=pltpu.HBM), pl.BlockSpec(memory_space=pl.ANY)],
        out_specs=[vm, vm],
        out_shape=[pltpu.VMEM(gate_weight.shape, BF), jax.ShapeDtypeStruct((8, 128), F32)],
        scratch_shapes=[pltpu.SemaphoreType.DMA((chunks,))],
        compiler_params=params(1),
        cost_estimate=cost(1e5, 1 << 12),
        name="load",
    )(in_hbm(gate_weight), y_own)
    anyspace = pl.BlockSpec(memory_space=pl.ANY)

    def add_core(keep, send, each, name, dep=()):
        got = trade(send, "core", 2, 1)
        shape = (n * each, wc)
        outs = [(shape, F32)] + [(shape, BF)] * (m - 1)
        return small(functools.partial(pair_rows_kernel, m), name, outs, (keep, got), dep)

    def send_z(parts):
        return [parts[0]] + [trade(parts[k], "z", m, k) for k in range(1, m)]

    def add_z(got, each, name, dep=()):
        outs = [((each, wc), BF)] * n
        out = small(functools.partial(sum_rows_kernel, len(got), n), name, outs, got, dep)
        return [out[0]] + [trade(out[k], "dp", n, k) for k in range(1, n)]

    keep_slot, send_slot_rows, keep_own, send_own = project(
        n, ys, sel_slot, sel_own, out_weight, loaded
    )
    parts = add_core(keep_slot, send_slot_rows, pe, "core_slot")
    slot_z = send_z(parts)
    hid = add_z(slot_z, pe, "z_slot")
    [normed] = small(
        functools.partial(norm_kernel, n),
        "norm",
        [((pe, dm), BF)],
        (me, norm_gain.reshape(1, dm), *hid),
    )
    near = [normed] + [trade(normed, "z", m, k) for k in range(1, m)]
    xs = []
    for piece in near:
        xs += [piece, trade(piece, "core", 2, 1)]
    size = m * n * rm // 2
    halves = [((size, wc), F32), ((size, wc), BF)]
    own_keep, own_send = small(
        functools.partial(pair_rows_kernel, 2),
        "core_own",
        halves,
        (keep_own, trade(send_own, "core", 2, 1)),
        (near[1],),
    )
    held = pl.pallas_call(
        hold_kernel,
        in_specs=[anyspace] * n,
        out_specs=[anyspace] * (n - 1),
        out_shape=[jax.ShapeDtypeStruct(k.shape, k.dtype) for k in kept[1:]],
        input_output_aliases={k: k for k in range(n - 1)},
        compiler_params=params(1),
        name="hold",
    )(*kept[1:], near[1])
    back = [kept[0]] + [trade(held[k - 1], "dp", n, k) for k in range(1, n)]

    half = dm // 2
    pc = half // m
    ub = 256 if width % 256 == 0 else 128
    act = pl.pallas_call(
        functools.partial(gate_kernel, m),
        in_specs=[sm] + [vm] * (2 * m + 2) + [pl.BlockSpec(memory_space=pltpu.HBM)],
        out_specs=vm,
        out_shape=jax.ShapeDtypeStruct((cap, width), BF),
        scratch_shapes=[
            pltpu.VMEM((cap, dm), BF),
            pltpu.VMEM((2, dm, ub), BF),
            pltpu.SemaphoreType.DMA((2,)),
        ],
        compiler_params=params(14),
        cost_estimate=cost(4 * cap * dm * width, 4 * dm * width),
        name="gate",
    )(me, *xs, share, gate_here, in_hbm(up_weight))
    k = m // 2
    while k > 1:
        size //= 2
        own_keep, own_send = small(
            functools.partial(pair_rows_kernel, 2),
            f"half{k}",
            [((size, wc), F32), ((size, wc), BF)],
            (own_keep, trade(own_send, "z", m, k)),
        )
        k //= 2
    own_z = [own_keep, trade(own_send, "z", m, 1)]
    deps = [own_send] + back[1:]
    send, keep = pl.pallas_call(
        functools.partial(down_kernel, m, len(deps)),
        in_specs=[sm, vm, pl.BlockSpec(memory_space=pltpu.HBM)] + [anyspace] * len(deps),
        out_specs=[vm] * 2,
        out_shape=[jax.ShapeDtypeStruct((cap, half), BF)] * 2,
        scratch_shapes=[pltpu.VMEM((6, width, pc // 2), BF), pltpu.SemaphoreType.DMA((6,))],
        compiler_params=params(14),
        cost_estimate=cost(2 * cap * dm * width, 2 * dm * width),
        name="down",
    )(me, act, in_hbm(down_weight), *deps)

    got = trade(send, "core", 2, 1)
    outs = [((cap, pc), F32)] + [((cap, pc), BF)] * (m - 1)
    cols = small(functools.partial(pair_cols_kernel, m), "core_out", outs, (keep, got))
    moved = [cols[0]] + [trade(cols[k], "z", m, k) for k in range(1, m)]

    own = add_z(own_z, rm, "z_own", (cols[1],))
    low = kept[0].shape[0] - per * states
    tail_at = per * states // low
    new_tail, tailed = pl.pallas_call(
        functools.partial(tail_kernel, n, per, taps),
        grid=(1,),
        in_specs=[sm, sm, pl.BlockSpec(x_input.shape, lambda g: (0, 0, 0))]
        + [pl.BlockSpec((low, ch), lambda g: (tail_at, 0))] * n
        + [anyspace],
        out_specs=[
            pl.BlockSpec((taps, rows, ch), lambda g: (0, 0, 0)),
            pl.BlockSpec((8, 128), lambda g: (0, 0)),
        ],
        out_shape=[
            jax.ShapeDtypeStruct((taps, rows, ch), F32),
            jax.ShapeDtypeStruct((8, 128), F32),
        ],
        compiler_params=params(8),
        cost_estimate=cost(1e5, 1 << 12),
        name="tail",
    )(me, rr, x_input, *back, cols[1])
    share_rows = total // n
    outs = [((share_rows, pc), F32)] + [((share_rows, pc), BF)] * (n - 1)
    rows_out = small(
        functools.partial(spread_kernel, n, m),
        "spread",
        outs,
        (me, expand, *moved),
        (tailed, *own[1:]),
        [pltpu.VMEM((total, pc), F32)],
    )
    new_state, placed = place(n, per, rows, states, me, rr, back, rows_out[1])

    mine = [rows_out[0]] + [trade(rows_out[k], "dp", n, k) for k in range(1, n)]
    deal_keep, deal_send = small(
        functools.partial(deal_kernel, n, m),
        "deal",
        [((m * rm, pc), BF)] * 2,
        (me, *mine),
        (placed,),
        [pltpu.VMEM((share_rows, pc), F32)],
    )
    pieces = small(
        functools.partial(pair_kernel, m),
        "pair",
        [((rm, 2 * pc), BF)] * m,
        (deal_keep, trade(deal_send, "core", 2, 1)),
    )
    pieces = send_z(pieces)
    [mixed] = small(
        functools.partial(final_kernel, n, m),
        "final",
        [((rm, dm), BF)],
        (me, *own, *pieces),
        (),
        [pltpu.VMEM((rm, dm), F32)],
    )
    return (mixed, new_state, jnp.transpose(new_tail, (1, 0, 2)))


def solution(mesh):
    n = mesh.shape["dp"]
    m = mesh.shape["expert"] // 2
    split = Mesh(mesh.devices.reshape(n, m, 2), ("dp", "z", "core"))
    e = ("z", "core")
    de = ("dp", "z", "core")
    in_specs = (
        P("dp", None, e),
        P("dp", None, e),
        P(),
        P("dp", None, None),
        P("dp"),
        P(None, "dp", e),
        P(None, "dp", e),
        P(None, "dp", e),
        P(None, "dp", None),
        P(None, "dp", None),
        P(None, e),
        P(e),
        P(e),
        P(None, e),
        P(e),
        P(e, "dp"),
        P(),
        P(),
        P(),
        P(),
        P(None, de),
        P(None, de),
        P(de, None),
    )
    out_specs = (P(de, None), P("dp", None, e), P("dp", None, e))
    return jax.shard_map(body, mesh=split, in_specs=in_specs, out_specs=out_specs, check_vma=False)
```
